32 devices in a mesh: win: 2 (over x), sta: 16 (over z, y, core).
Axes of the slice: x: 2, y: 2, z: 4, core: 2. Of those that a mesh axis runs over, the one named last changes fastest.
Arguments:
- samples: bfloat16 [256, 1048576], P('sta', 'win'), may hold values from -6 to 6
- coarse_taps: bfloat16 [16, 512], replicated, may hold values from -0.0625 to 0.0625
- fine_taps: bfloat16 [8, 64], replicated, may hold values from -0.25 to 0.25
Outputs:
- visibilities: bfloat16 [128, 64, 2, 256, 256], P('win', 'sta')
The draws below stay inside these ranges and needn't reach their ends.
All inputs are finite; a program needn't handle non-finite values.
Results may differ from the reference program's by a relative error of at most 0.008.
Values may be sent and summed in bfloat16 or wider, within the bound.
No kernel may reach another device: no remote copies, remote signals or barrier semaphores. Data moves between devices by JAX's collectives and lax.ppermute only.
A program may use at most 320 MiB of HBM per device.

```python
import math
import jax
import jax.numpy as jnp
from jax import lax

SIG = 256
FRAME = 512
KEEP = 128
FIRST = 64
TAPS = 16
FINE = 64
FTAPS = 8
NT = 1048576


def block_levels(rng, shape, cuts, smallest, high):
    def one(dim, shards_of):
        heights = jax.random.uniform(jax.random.fold_in(jax.random.fold_in(rng, 6), dim), (shards_of,), jnp.float32, smallest / len(cuts), high / len(cuts))
        return jnp.repeat(jnp.exp(heights), shape[dim] // shards_of).reshape((-1,) + (1,) * (len(shape) - dim - 1))

    gain = one(*cuts[0])
    for cut in cuts[1:]:
        gain = gain * one(*cut)
    return gain


def noise(key, dims, width, limit, pieces=(), kind=jnp.bfloat16):
    factor_of = block_levels(key, dims, pieces, -0.22, 0.18) if pieces else 1.0
    drawn = jax.random.normal(key, dims, jnp.float32) * width * factor_of
    return jnp.minimum(jnp.maximum(drawn, -limit), limit).astype(kind)


def setup_inputs(seed: int = 0) -> dict:
    keys = jax.random.split(jax.random.key(seed), 4)
    samples = noise(keys[0], (SIG, NT), 1.0, 6.0, ((0, 16), (1, 2)))
    coarse_taps = noise(keys[1], (TAPS, FRAME), (TAPS * FRAME) ** -0.5, 0.0625)
    fine_taps = noise(keys[2], (FTAPS, FINE), (FTAPS * FINE) ** -0.5, 0.25)
    return dict(samples=samples, coarse_taps=coarse_taps, fine_taps=fine_taps)


def coarse_matrix():
    channels = FIRST + jnp.arange(KEEP, dtype=jnp.int32)
    products = jnp.arange(FRAME, dtype=jnp.int32)[:, None] * channels[None, :]
    angles = (products % FRAME).astype(jnp.float32) * (2.0 * math.pi / FRAME)
    return jnp.concatenate([jnp.cos(angles), -jnp.sin(angles)], axis=1).astype(jnp.bfloat16)


def fine_tables():
    products = jnp.arange(FINE, dtype=jnp.int32)[:, None] * jnp.arange(FINE, dtype=jnp.int32)[None, :]
    angles = (products % FINE).astype(jnp.float32) * (2.0 * math.pi / FINE)
    return jnp.cos(angles), jnp.sin(angles)


def channelise(signal, coarse_taps, fine_taps, coarse_dft, cosines, sines):
    frame_count = NT // FRAME
    frames_all = signal.reshape(frame_count, FRAME)
    padded = jnp.concatenate([jnp.zeros((TAPS - 1, FRAME), jnp.bfloat16), frames_all], axis=0)
    windowed = jnp.zeros((frame_count, FRAME), jnp.float32)
    for tap_index in range(TAPS):
        start = TAPS - 1 - tap_index
        windowed = windowed + coarse_taps[tap_index].astype(jnp.float32)[None, :] * padded[start:start + frame_count].astype(jnp.float32)
    spectra = jnp.dot(windowed.astype(jnp.bfloat16), coarse_dft, preferred_element_type=jnp.float32).astype(jnp.bfloat16)
    history = (FTAPS - 1) * FINE
    extended = jnp.concatenate([jnp.zeros((history, 2 * KEEP), jnp.bfloat16), spectra], axis=0)
    fine_count = frame_count // FINE
    groups = extended.reshape(fine_count + FTAPS - 1, FINE, 2, KEEP)
    filtered = jnp.zeros((fine_count, FINE, 2, KEEP), jnp.float32)
    for tap_index in range(FTAPS):
        start = FTAPS - 1 - tap_index
        filtered = filtered + fine_taps[tap_index].astype(jnp.float32)[None, :, None, None] * groups[start:start + fine_count].astype(jnp.float32)
    real_part = filtered[:, :, 0]
    imag_part = filtered[:, :, 1]
    highest = lax.Precision.HIGHEST
    out_real = jnp.einsum("qj,gjk->kqg", cosines, real_part, precision=highest) + jnp.einsum("qj,gjk->kqg", sines, imag_part, precision=highest)
    out_imag = jnp.einsum("qj,gjk->kqg", cosines, imag_part, precision=highest) - jnp.einsum("qj,gjk->kqg", sines, real_part, precision=highest)
    return jnp.stack([out_real, out_imag], axis=2).astype(jnp.bfloat16)


def reference(samples, coarse_taps, fine_taps):
    coarse_dft = coarse_matrix()
    cosines, sines = fine_tables()
    spectra_all = lax.map(lambda signal: channelise(signal, coarse_taps, fine_taps, coarse_dft, cosines, sines), samples)
    frame_total = NT // (FRAME * FINE)
    highest = lax.Precision.HIGHEST

    def correlate(channel):
        channel_block = lax.dynamic_index_in_dim(spectra_all, channel, 1, keepdims=False).astype(jnp.float32)
        channel_block = jnp.transpose(channel_block, (1, 0, 2, 3))
        columns_all = channel_block.reshape(FINE, SIG, 2 * frame_total)
        turned = jnp.concatenate([channel_block[:, :, 1], -channel_block[:, :, 0]], axis=2)
        real_vis = jnp.einsum("qsc,qtc->qst", columns_all, columns_all, precision=highest)
        imag_vis = jnp.einsum("qsc,qtc->qst", turned, columns_all, precision=highest)
        return (jnp.stack([real_vis, imag_vis], axis=1) / frame_total).astype(jnp.bfloat16)

    return lax.map(correlate, jnp.arange(KEEP, dtype=jnp.int32))
```

```python
import functools
import math

import jax
import jax.numpy as jnp
from jax import lax
from jax.experimental import pallas as pl
from jax.experimental.pallas import tpu as pltpu
from jax.sharding import PartitionSpec as P

KEEP = 128
LANES = 128
ROWS = 16
BLOCK = 128


def from_behind(x, axis, by):
    size = lax.axis_size(axis)
    pairs = [(i, i + by) for i in range(size) if 0 <= i + by < size]
    return lax.ppermute(x, axis, pairs)


def coarse_matrix(frame_len, band_count):
    channels = frame_len // 8 + jnp.arange(band_count, dtype=jnp.int32)
    products = jnp.arange(frame_len, dtype=jnp.int32)[:, None] * channels[None, :]
    angles = (products % frame_len).astype(jnp.float32) * (2.0 * math.pi / frame_len)
    return jnp.concatenate([jnp.cos(angles), -jnp.sin(angles)], axis=1).astype(jnp.bfloat16)


def fine_tables(fine_len):
    products = (
        jnp.arange(fine_len, dtype=jnp.int32)[:, None]
        * jnp.arange(fine_len, dtype=jnp.int32)[None, :]
    )
    angles = (products % fine_len).astype(jnp.float32) * (2.0 * math.pi / fine_len)
    return (jnp.cos(angles), jnp.sin(angles))


def correlate(spectra_in, pieces):
    band_local, fine_local, sig_count, columns = spectra_in.shape
    split_view = spectra_in.reshape(
        band_local, fine_local, sig_count, pieces, 2, columns // (2 * pieces)
    )
    turned = jnp.stack([split_view[:, :, :, :, 1], -split_view[:, :, :, :, 0]], axis=4).reshape(
        band_local, fine_local, sig_count, columns
    )
    real_vis = jnp.einsum(
        "kqsc,kqtc->kqst", spectra_in, spectra_in, preferred_element_type=jnp.float32
    )
    imag_vis = jnp.einsum("kqsc,kqtc->kqst", turned, spectra_in, preferred_element_type=jnp.float32)
    return jnp.stack([real_vis, imag_vis], axis=2)


def per_device_general(samples, coarse_taps, fine_taps):
    sig_local, samp_local = samples.shape
    tap_count, frame_len = coarse_taps.shape
    fine_tap_count, fine_len = fine_taps.shape
    band_count = KEEP
    frame_count = samp_local // frame_len
    frames_local = samples.reshape(sig_local, frame_count, frame_len)
    earlier = from_behind(frames_local[:, frame_count - (tap_count - 1) :], "win", 1)
    padded = jnp.concatenate([earlier, frames_local], axis=1)
    windowed = jnp.zeros((sig_local, frame_count, frame_len), jnp.float32)
    for tap_index in range(tap_count):
        start = tap_count - 1 - tap_index
        windowed = windowed + coarse_taps[tap_index].astype(jnp.float32)[None, None, :] * padded[
            :, start : start + frame_count
        ].astype(jnp.float32)
    spectra = jnp.dot(
        windowed.astype(jnp.bfloat16).reshape(sig_local * frame_count, frame_len),
        coarse_matrix(frame_len, band_count),
        preferred_element_type=jnp.float32,
    )
    spectra = spectra.astype(jnp.bfloat16).reshape(sig_local, frame_count, 2 * band_count)
    history = (fine_tap_count - 1) * fine_len
    carried = from_behind(spectra[:, frame_count - history :], "win", 1)
    extended = jnp.concatenate([carried, spectra], axis=1)
    fine_count = frame_count // fine_len
    groups = extended.reshape(sig_local, fine_count + fine_tap_count - 1, fine_len, 2, band_count)
    filtered = jnp.zeros((sig_local, fine_count, fine_len, 2, band_count), jnp.float32)
    for tap_index in range(fine_tap_count):
        start = fine_tap_count - 1 - tap_index
        filtered = filtered + fine_taps[tap_index].astype(jnp.float32)[
            None, None, :, None, None
        ] * groups[:, start : start + fine_count].astype(jnp.float32)
    cosines, sines = fine_tables(fine_len)
    real_part = filtered[:, :, :, 0]
    imag_part = filtered[:, :, :, 1]
    highest = lax.Precision.HIGHEST
    out_real = jnp.einsum("qj,sgjk->kqsg", cosines, real_part, precision=highest) + jnp.einsum(
        "qj,sgjk->kqsg", sines, imag_part, precision=highest
    )
    out_imag = jnp.einsum("qj,sgjk->kqsg", cosines, imag_part, precision=highest) - jnp.einsum(
        "qj,sgjk->kqsg", sines, real_part, precision=highest
    )
    local_spectra = (
        jnp.stack([out_real, out_imag], axis=3)
        .astype(jnp.bfloat16)
        .reshape(band_count, fine_len, sig_local, 2 * fine_count)
    )
    frame_total = fine_count * lax.axis_size("win")
    moved = lax.all_to_all(local_spectra, "sta", split_axis=1, concat_axis=2, tiled=True)
    moved = lax.all_to_all(moved, "win", split_axis=0, concat_axis=3, tiled=True)
    vis_local = correlate(moved, lax.axis_size("win"))
    return (vis_local / frame_total).astype(jnp.bfloat16)


def swap(x, axis, by):
    return lax.ppermute(x, axis, [(i, i ^ by) for i in range(lax.axis_size(axis))])


def coarse_rows(frame_len, band_half, chunks):
    half = lax.axis_index("win")
    rows = []
    for h in range(2):
        base = 0
        for size in chunks:
            for part in range(2):
                channel = (half ^ h) * band_half + base + jnp.arange(size, dtype=jnp.int32)
                rows.append(channel * 2 + part)
            base += size
    code = jnp.concatenate(rows)
    channel = frame_len // 8 + code // 2
    products = channel[:, None] * jnp.arange(frame_len, dtype=jnp.int32)[None, :]
    angles = (products % frame_len).astype(jnp.float32) * (2.0 * math.pi / frame_len)
    return jnp.where((code % 2 == 0)[:, None], jnp.cos(angles), -jnp.sin(angles)).astype(jnp.bfloat16)


def coarse_kernel(chunks, taps_n, x_ref, before_ref, hist_ref, taps_ref, dft_ref, *refs):
    outs, (xs, wd) = refs[:-2], refs[-2:]
    step = pl.program_id(0)
    keep = taps_n - 1
    pieces = xs.shape[1]
    skip = before_ref.shape[1] // (pieces * LANES) - keep
    group = 8

    def halves(v):
        return v.astype(jnp.float32).reshape(2, 8, LANES)

    @pl.when(step == 0)
    def _():
        for f in range(keep):
            for j in range(pieces):
                xs[f, j] = halves(hist_ref[:, (f * pieces + j) * LANES : (f * pieces + j + 1) * LANES])

    @pl.when(step > 0)
    def _():
        for f in range(keep):
            for j in range(pieces):
                at = ((f + skip) * pieces + j) * LANES
                xs[f, j] = halves(before_ref[:, at : at + LANES])

    def widen(f, _):
        for j in range(pieces):
            at = pl.multiple_of((f * pieces + j) * LANES, LANES)
            xs[keep + f, j] = halves(x_ref[:, pl.ds(at, LANES)])
        return 0

    lax.fori_loop(0, BLOCK, widen, 0, unroll=4)

    for j in range(pieces):
        taps = [taps_ref[j, m] for m in range(taps_n)]

        def fir(b, _):
            first = b * group
            for h in range(2):
                xv = [xs[first + t, j, h] for t in range(group + keep)]
                for g in range(group):
                    acc = taps[0] * xv[g + keep]
                    for m in range(1, taps_n):
                        acc = acc + taps[m] * xv[g + keep - m]
                    wd[j, pl.ds(pl.multiple_of((first + g) * ROWS + h * 8, 8), 8), :] = acc
            return 0

        lax.fori_loop(0, BLOCK // group, fir, 0)

    def project(p, _):
        rows = []
        for t in range(2):
            parts = [wd[j, pl.ds(2 * p + t, BLOCK, stride=ROWS), :] for j in range(pieces)]
            rows.append(jnp.concatenate(parts, axis=1).astype(jnp.bfloat16))
        both = jnp.concatenate(rows, axis=0)
        res = lax.dot_general(
            dft_ref[...], both, (((1,), (1,)), ((), ())), preferred_element_type=jnp.float32
        ).astype(jnp.bfloat16)
        for t in range(2):
            base = 0
            for n, out in enumerate(outs):
                size = 2 * chunks[n % len(chunks)]
                out[2 * p + t] = res[base : base + size, t * BLOCK : (t + 1) * BLOCK]
                base += size
        return 0

    lax.fori_loop(0, ROWS // 2, project, 0)


def coarse(samples, hist, coarse_taps, dft, chunks):
    sig, samp = samples.shape
    taps_n, frame_len = coarse_taps.shape
    pieces = frame_len // LANES
    frames = samp // frame_len
    before = taps_n
    taps = jnp.broadcast_to(
        coarse_taps.astype(jnp.float32).reshape(taps_n, pieces, LANES).transpose(1, 0, 2)[:, :, None],
        (pieces, taps_n, 8, LANES),
    )
    ratio = BLOCK // before
    shapes = [jax.ShapeDtypeStruct((sig, 2 * c, frames), jnp.bfloat16) for c in chunks * 2]
    return pl.pallas_call(
        functools.partial(coarse_kernel, chunks, taps_n),
        grid=(frames // BLOCK,),
        in_specs=[
            pl.BlockSpec((sig, BLOCK * frame_len), lambda i: (0, i)),
            pl.BlockSpec((sig, before * frame_len), lambda i: (0, jnp.maximum(i * ratio - 1, 0))),
            pl.BlockSpec(hist.shape, lambda i: (0, 0)),
            pl.BlockSpec(taps.shape, lambda i: (0, 0, 0, 0)),
            pl.BlockSpec(dft.shape, lambda i: (0, 0)),
        ],
        out_specs=[pl.BlockSpec((sig, 2 * c, BLOCK), lambda i: (0, 0, i)) for c in chunks * 2],
        out_shape=shapes,
        scratch_shapes=[
            pltpu.VMEM((BLOCK + taps_n - 1, pieces, 2, 8, LANES), jnp.float32),
            pltpu.VMEM((pieces, BLOCK * ROWS, LANES), jnp.float32),
        ],
        compiler_params=pltpu.CompilerParams(vmem_limit_bytes=50 << 20),
        cost_estimate=pl.CostEstimate(
            flops=2 * sig * frames * frame_len * (dft.shape[0] + 128 * taps_n),
            bytes_accessed=2 * sig * samp * 2,
            transcendentals=0,
        ),
    )(samples, samples, hist, taps, dft)


def fine_kernel(low, own_ref, oth_ref, town_ref, toth_ref, cos_ref, sin_ref, *refs):
    outs, zs = refs[:-1], refs[-1]
    sig, two_c, frames = own_ref.shape
    size = two_c // 2
    r = pl.program_id(0)
    cos, sin = cos_ref[...], sin_ref[...]

    def table(t_ref):
        t = t_ref[...]
        return jnp.concatenate(
            [(t * w).astype(jnp.bfloat16).reshape(frames, LANES) for w in (cos, sin)], axis=1
        )

    acc = jnp.dot(
        own_ref[...].reshape(sig * two_c, frames), table(town_ref), preferred_element_type=jnp.float32
    ) + jnp.dot(
        oth_ref[...].reshape(sig * two_c, frames), table(toth_ref), preferred_element_type=jnp.float32
    )
    acc = acc.reshape(sig, 2, size, 2 * LANES)
    p, q = acc[..., :LANES], acc[..., LANES:]
    view = zs.reshape(sig, 2, size, LANES)
    view[:, 0] = p[:, 0] + q[:, 1]
    view[:, 1] = p[:, 1] - q[:, 0]
    for n, out in enumerate(outs):

        @pl.when(r // low == n)
        def _(out=out):
            for c in range(size):
                for part in range(2):
                    out[0, c, part] = zs[pl.ds(part * size + c, sig, stride=two_c), :].astype(
                        jnp.bfloat16
                    )


def fine(own, oth, town, toth, cos, sin, low):
    sig, two_c, frames = own.shape
    dests = cos.shape[0]
    unit = (two_c // 2, 2, sig, LANES)
    highs = dests // low

    def place(n):
        return lambda r: (jnp.clip(r - n * low, 0, low - 1), 0, 0, 0, 0)

    return pl.pallas_call(
        functools.partial(fine_kernel, low),
        grid=(dests,),
        in_specs=[
            pl.BlockSpec(own.shape, lambda r: (0, 0, 0)),
            pl.BlockSpec(oth.shape, lambda r: (0, 0, 0)),
            pl.BlockSpec(town.shape, lambda r: (0, 0, 0)),
            pl.BlockSpec(toth.shape, lambda r: (0, 0, 0)),
            pl.BlockSpec((1,) + cos.shape[1:], lambda r: (r, 0, 0)),
            pl.BlockSpec((1,) + sin.shape[1:], lambda r: (r, 0, 0)),
        ],
        out_specs=[pl.BlockSpec((1,) + unit, place(n)) for n in range(highs)],
        out_shape=[jax.ShapeDtypeStruct((low,) + unit, jnp.bfloat16) for n in range(highs)],
        scratch_shapes=[pltpu.VMEM((sig * two_c, LANES), jnp.float32)],
        compiler_params=pltpu.CompilerParams(vmem_limit_bytes=50 << 20),
        cost_estimate=pl.CostEstimate(
            flops=2 * sig * two_c * 2 * frames * dests * 2 * LANES,
            bytes_accessed=6 * sig * two_c * frames,
            transcendentals=0,
        ),
    )(own, oth, town, toth, cos, sin)


def correlate_kernel(sources, scale, per_q, me_ref, *refs):
    ins, out, xr, xi = refs[: len(sources)], refs[-3], refs[-2], refs[-1]
    me = me_ref[0]
    for ref, units in zip(ins, sources):
        for at, rel in units:
            row = pl.multiple_of((me ^ rel) * ROWS, ROWS)
            xr[pl.ds(row, ROWS), :] = ref[at + (0, 0)]
            xi[pl.ds(row, ROWS), :] = ref[at + (0, 1)]
    re, im = xr[...], xi[...]
    left = jnp.concatenate([re, im], axis=1)
    lane = lax.broadcasted_iota(jnp.int32, (1, LANES), 1)
    dims = (((1,), (1,)), ((), ()))
    for q in range(LANES // per_q):
        pick = lane // per_q == q
        zero = jnp.zeros((), jnp.bfloat16)
        rq, iq = jnp.where(pick, re, zero), jnp.where(pick, im, zero)
        real = lax.dot_general(
            left, jnp.concatenate([rq, iq], axis=1), dims, preferred_element_type=jnp.float32
        )
        imag = lax.dot_general(
            left, jnp.concatenate([-iq, rq], axis=1), dims, preferred_element_type=jnp.float32
        )
        out[0, q, 0] = (real * scale).astype(jnp.bfloat16)
        out[0, q, 1] = (imag * scale).astype(jnp.bfloat16)


def correlate_chunk(me, arrays, leads, sources, whole, offset, shape, per_q, scale):
    size = arrays[0].shape[-4]
    signals = shape[-1]
    specs = [pl.BlockSpec(memory_space=pltpu.SMEM)]
    for a, lead in zip(arrays, leads):
        specs.append(
            pl.BlockSpec(
                tuple(lead) + (1,) + a.shape[-3:],
                lambda c, n=len(lead): (0,) * n + (c, 0, 0, 0),
            )
        )
    operands = [me] + list(arrays)
    alias = {}
    if whole is not None:
        alias = {len(operands): 0}
        specs.append(pl.BlockSpec(memory_space=pl.ANY))
        operands.append(whole)
    return pl.pallas_call(
        functools.partial(correlate_kernel, sources, scale, per_q),
        grid=(size,),
        in_specs=specs,
        out_specs=pl.BlockSpec((1,) + shape[1:], lambda c: (c + offset, 0, 0, 0, 0)),
        out_shape=jax.ShapeDtypeStruct(shape, jnp.bfloat16),
        scratch_shapes=[pltpu.VMEM((signals, LANES), jnp.bfloat16)] * 2,
        input_output_aliases=alias,
        compiler_params=pltpu.CompilerParams(vmem_limit_bytes=40 << 20),
        cost_estimate=pl.CostEstimate(
            flops=size * 8 * signals * signals * 4 * LANES,
            bytes_accessed=size * 2 * math.prod(shape[1:]),
            transcendentals=0,
        ),
    )(*operands)


def chunk_sizes(channels):
    return [channels // 4] * 4


def per_device(samples, coarse_taps, fine_taps):
    sig, samp = samples.shape
    taps_n, frame_len = coarse_taps.shape
    ftaps_n, fine_len = fine_taps.shape
    dests = lax.axis_size("sta")
    me = lax.axis_index("sta")
    win = lax.axis_index("win")
    frames = samp // frame_len
    fine_local = frames // fine_len
    total = fine_local * 2
    per_dest = fine_len // dests
    channels = KEEP // 2
    chunks = chunk_sizes(channels)
    low = 4

    hist = from_behind(samples[:, samp - (taps_n - 1) * frame_len :], "win", 1)
    dft = coarse_rows(frame_len, channels, chunks)
    parts = coarse(samples, hist, coarse_taps, dft, chunks)
    own, away = parts[: len(chunks)], parts[len(chunks) :]

    lane = jnp.arange(LANES, dtype=jnp.int32)
    frame_of = lane % total
    weights = fine_taps.astype(jnp.float32)

    def taps_table(side):
        block = side * fine_local + jnp.arange(fine_local, dtype=jnp.int32)
        late = frame_of[None, :] - block[:, None]
        table = jnp.zeros((fine_local, fine_len, LANES), jnp.float32)
        for m in range(ftaps_n):
            table = table + jnp.where((late == m)[:, None, :], weights[m][None, :, None], 0.0)
        return table

    town, toth = taps_table(win), taps_table(1 - win)
    fine_of = (me ^ jnp.arange(dests, dtype=jnp.int32))[:, None] * per_dest + (lane // total)[None, :]
    turns = fine_of[:, None, :] * jnp.arange(fine_len, dtype=jnp.int32)[None, :, None]
    angles = (turns % fine_len).astype(jnp.float32) * (2.0 * math.pi / fine_len)
    cos, sin = jnp.cos(angles), jnp.sin(angles)

    shape = (channels, per_dest, 2, sig * dests, sig * dests)
    result, offset = None, 0
    for k, size in enumerate(chunks):
        oth = swap(away[k], "win", 1)
        sent = fine(own[k], oth, town, toth, cos, sin, low)
        held = [sent[0]] + [swap(s, "sta", low * n) for n, s in enumerate(sent) if n]
        over = swap(jnp.stack([h[2:] for h in held]), "sta", 2)
        last = swap(jnp.stack([jnp.stack([h[1] for h in held]), over[:, 1]]), "sta", 1)
        highs = range(len(held))
        arrays = list(held) + [over, last]
        leads = [(1,)] * len(held) + [(len(held), 1), last.shape[:2]]
        sources = [[((0,), low * n)] for n in highs]
        sources.append([((n, 0), low * n + 2) for n in highs])
        sources.append([((y, n), low * n + 2 * y + 1) for y in range(2) for n in highs])
        result = correlate_chunk(
            me[None].astype(jnp.int32), arrays, leads, sources, result, offset, shape, total, 1.0 / total
        )
        offset += size
    return result


def solution(mesh):
    placed = (P("sta", "win"), P(), P())
    fits = mesh.shape["win"] == 2 and mesh.shape["sta"] == 16
    return jax.shard_map(
        per_device if fits else per_device_general,
        mesh=mesh,
        in_specs=placed,
        out_specs=P("win", "sta", None, None, None),
        check_vma=False,
    )
```

```python
import functools
import math

import jax
import jax.numpy as jnp
from jax import lax
from jax.experimental import pallas as pl
from jax.experimental.pallas import tpu as pltpu
from jax.sharding import PartitionSpec as P

KEEP = 128
LANES = 128
WIDE = 256
PITCH = 17
ROWS = 16
BLOCK = 128


def from_behind(x, axis, by):
    size = lax.axis_size(axis)
    pairs = [(i, i + by) for i in range(size) if 0 <= i + by < size]
    return lax.ppermute(x, axis, pairs)


def coarse_matrix(frame_len, band_count):
    channels = frame_len // 8 + jnp.arange(band_count, dtype=jnp.int32)
    products = jnp.arange(frame_len, dtype=jnp.int32)[:, None] * channels[None, :]
    angles = (products % frame_len).astype(jnp.float32) * (2.0 * math.pi / frame_len)
    return jnp.concatenate([jnp.cos(angles), -jnp.sin(angles)], axis=1).astype(jnp.bfloat16)


def fine_tables(fine_len):
    products = (
        jnp.arange(fine_len, dtype=jnp.int32)[:, None]
        * jnp.arange(fine_len, dtype=jnp.int32)[None, :]
    )
    angles = (products % fine_len).astype(jnp.float32) * (2.0 * math.pi / fine_len)
    return (jnp.cos(angles), jnp.sin(angles))


def correlate(spectra_in, pieces):
    band_local, fine_local, sig_count, columns = spectra_in.shape
    split_view = spectra_in.reshape(
        band_local, fine_local, sig_count, pieces, 2, columns // (2 * pieces)
    )
    turned = jnp.stack([split_view[:, :, :, :, 1], -split_view[:, :, :, :, 0]], axis=4).reshape(
        band_local, fine_local, sig_count, columns
    )
    real_vis = jnp.einsum(
        "kqsc,kqtc->kqst", spectra_in, spectra_in, preferred_element_type=jnp.float32
    )
    imag_vis = jnp.einsum("kqsc,kqtc->kqst", turned, spectra_in, preferred_element_type=jnp.float32)
    return jnp.stack([real_vis, imag_vis], axis=2)


def per_device_general(samples, coarse_taps, fine_taps):
    sig_local, samp_local = samples.shape
    tap_count, frame_len = coarse_taps.shape
    fine_tap_count, fine_len = fine_taps.shape
    band_count = KEEP
    frame_count = samp_local // frame_len
    frames_local = samples.reshape(sig_local, frame_count, frame_len)
    earlier = from_behind(frames_local[:, frame_count - (tap_count - 1) :], "win", 1)
    padded = jnp.concatenate([earlier, frames_local], axis=1)
    windowed = jnp.zeros((sig_local, frame_count, frame_len), jnp.float32)
    for tap_index in range(tap_count):
        start = tap_count - 1 - tap_index
        windowed = windowed + coarse_taps[tap_index].astype(jnp.float32)[None, None, :] * padded[
            :, start : start + frame_count
        ].astype(jnp.float32)
    spectra = jnp.dot(
        windowed.astype(jnp.bfloat16).reshape(sig_local * frame_count, frame_len),
        coarse_matrix(frame_len, band_count),
        preferred_element_type=jnp.float32,
    )
    spectra = spectra.astype(jnp.bfloat16).reshape(sig_local, frame_count, 2 * band_count)
    history = (fine_tap_count - 1) * fine_len
    carried = from_behind(spectra[:, frame_count - history :], "win", 1)
    extended = jnp.concatenate([carried, spectra], axis=1)
    fine_count = frame_count // fine_len
    groups = extended.reshape(sig_local, fine_count + fine_tap_count - 1, fine_len, 2, band_count)
    filtered = jnp.zeros((sig_local, fine_count, fine_len, 2, band_count), jnp.float32)
    for tap_index in range(fine_tap_count):
        start = fine_tap_count - 1 - tap_index
        filtered = filtered + fine_taps[tap_index].astype(jnp.float32)[
            None, None, :, None, None
        ] * groups[:, start : start + fine_count].astype(jnp.float32)
    cosines, sines = fine_tables(fine_len)
    real_part = filtered[:, :, :, 0]
    imag_part = filtered[:, :, :, 1]
    highest = lax.Precision.HIGHEST
    out_real = jnp.einsum("qj,sgjk->kqsg", cosines, real_part, precision=highest) + jnp.einsum(
        "qj,sgjk->kqsg", sines, imag_part, precision=highest
    )
    out_imag = jnp.einsum("qj,sgjk->kqsg", cosines, imag_part, precision=highest) - jnp.einsum(
        "qj,sgjk->kqsg", sines, real_part, precision=highest
    )
    local_spectra = (
        jnp.stack([out_real, out_imag], axis=3)
        .astype(jnp.bfloat16)
        .reshape(band_count, fine_len, sig_local, 2 * fine_count)
    )
    frame_total = fine_count * lax.axis_size("win")
    moved = lax.all_to_all(local_spectra, "sta", split_axis=1, concat_axis=2, tiled=True)
    moved = lax.all_to_all(moved, "win", split_axis=0, concat_axis=3, tiled=True)
    vis_local = correlate(moved, lax.axis_size("win"))
    return (vis_local / frame_total).astype(jnp.bfloat16)


def swap(x, axis, by):
    return lax.ppermute(x, axis, [(i, i ^ by) for i in range(lax.axis_size(axis))])


def coarse_rows(frame_len, band_half, chunks):
    half = lax.axis_index("win")
    rows = []
    for h in range(2):
        base = 0
        for size in chunks:
            for part in range(2):
                channel = (half ^ h) * band_half + base + jnp.arange(size, dtype=jnp.int32)
                rows.append(channel * 2 + part)
            base += size
    code = jnp.concatenate(rows)
    channel = frame_len // 8 + code // 2
    products = channel[:, None] * jnp.arange(frame_len, dtype=jnp.int32)[None, :]
    angles = (products % frame_len).astype(jnp.float32) * (2.0 * math.pi / frame_len)
    return jnp.where((code % 2 == 0)[:, None], jnp.cos(angles), -jnp.sin(angles)).astype(jnp.bfloat16)


def coarse_kernel(chunks, taps_n, x_ref, before_ref, hist_ref, taps_ref, dft_ref, *refs):
    outs, (xs, even, odd) = refs[:-3], refs[-3:]
    step, last = pl.program_id(0), pl.num_programs(0) - 1
    keep = taps_n - 1
    pieces = xs.shape[1]
    skip = before_ref.shape[1] // (pieces * WIDE) - keep
    group = 8

    def load():
        @pl.when(step == 0)
        def _():
            for f in range(keep):
                for j in range(pieces):
                    at = (f * pieces + j) * WIDE
                    xs[f, j] = hist_ref[:, at : at + WIDE]

        @pl.when(step > 0)
        def _():
            for f in range(keep):
                for j in range(pieces):
                    at = ((f + skip) * pieces + j) * WIDE
                    xs[f, j] = before_ref[:, at : at + WIDE]

        def move(f, _):
            for j in range(pieces):
                at = pl.multiple_of((f * pieces + j) * WIDE, WIDE)
                xs[keep + f, j] = x_ref[:, pl.ds(at, WIDE)]
            return 0

        lax.fori_loop(0, BLOCK, move, 0, unroll=8)

    def fir(wd, first, j):
        taps = [taps_ref[j, m] for m in range(taps_n)]
        xv = [xs[first + t, j] for t in range(group + keep)]
        for g in range(group):
            terms = [taps[m] * xv[g + keep - m] for m in range(taps_n)]
            for _ in range(2):
                terms = [a + b for a, b in zip(terms[::2], terms[1::2])]
            wide = [t.astype(jnp.float32) for t in terms]
            while len(wide) > 1:
                wide = [a + b for a, b in zip(wide[::2], wide[1::2])]
            rows = pl.ds((first + g) * PITCH, ROWS)
            for n in range(WIDE // LANES):
                wd[j * (WIDE // LANES) + n, rows, :] = wide[0][:, n * LANES : (n + 1) * LANES]

    def project(wd, p):
        rows = []
        for t in range(2):
            parts = [wd[j, pl.ds(2 * p + t, BLOCK, stride=PITCH), :] for j in range(wd.shape[0])]
            rows.append(jnp.concatenate(parts, axis=1).astype(jnp.bfloat16))
        both = jnp.concatenate(rows, axis=0)
        res = lax.dot_general(
            dft_ref[...], both, (((1,), (1,)), ((), ())), preferred_element_type=jnp.float32
        ).astype(jnp.bfloat16)
        for t in range(2):
            base = 0
            for n, out in enumerate(outs):
                size = 2 * chunks[n % len(chunks)]
                out[2 * p + t] = res[base : base + size, t * BLOCK : (t + 1) * BLOCK]
                base += size

    pairs = ROWS // 2
    share = BLOCK // pairs // group

    def run(fill, drain):
        def body(p, _):
            if drain is not None:
                project(drain, p)
            if fill is not None:
                for n in range(share):
                    for j in range(pieces):
                        fir(fill, (p * share + n) * group, j)
            return 0

        if fill is not None:
            load()
        lax.fori_loop(0, pairs, body, 0)

    @pl.when(step == 0)
    def _():
        run(even, None)

    @pl.when((step > 0) & (step < last) & (step % 2 == 1))
    def _():
        run(odd, even)

    @pl.when((step > 0) & (step < last) & (step % 2 == 0))
    def _():
        run(even, odd)

    @pl.when((step == last) & (step % 2 == 1))
    def _():
        run(None, even)

    @pl.when((step == last) & (step % 2 == 0))
    def _():
        run(None, odd)


def coarse(samples, hist, coarse_taps, dft, chunks):
    sig, samp = samples.shape
    taps_n, frame_len = coarse_taps.shape
    pieces = frame_len // WIDE
    frames = samp // frame_len
    before = taps_n
    taps = jnp.broadcast_to(
        coarse_taps.reshape(taps_n, pieces, WIDE).transpose(1, 0, 2)[:, :, None],
        (pieces, taps_n, ROWS, WIDE),
    )
    ratio = BLOCK // before
    blocks = frames // BLOCK
    shapes = [jax.ShapeDtypeStruct((sig, 2 * c, frames), jnp.bfloat16) for c in chunks * 2]

    def at(i):
        return jnp.minimum(i, blocks - 1)

    return pl.pallas_call(
        functools.partial(coarse_kernel, chunks, taps_n),
        grid=(blocks + 1,),
        in_specs=[
            pl.BlockSpec((sig, BLOCK * frame_len), lambda i: (0, at(i))),
            pl.BlockSpec((sig, before * frame_len), lambda i: (0, jnp.maximum(at(i) * ratio - 1, 0))),
            pl.BlockSpec(hist.shape, lambda i: (0, 0)),
            pl.BlockSpec(taps.shape, lambda i: (0, 0, 0, 0)),
            pl.BlockSpec(dft.shape, lambda i: (0, 0)),
        ],
        out_specs=[
            pl.BlockSpec((sig, 2 * c, BLOCK), lambda i: (0, 0, jnp.maximum(i - 1, 0)))
            for c in chunks * 2
        ],
        out_shape=shapes,
        scratch_shapes=[pltpu.VMEM((BLOCK + taps_n - 1, pieces, sig, WIDE), jnp.bfloat16)]
        + [pltpu.VMEM((frame_len // LANES, BLOCK * PITCH, LANES), jnp.float32)] * 2,
        compiler_params=pltpu.CompilerParams(vmem_limit_bytes=50 << 20),
        cost_estimate=pl.CostEstimate(
            flops=2 * sig * frames * frame_len * (dft.shape[0] + 128 * taps_n),
            bytes_accessed=2 * sig * samp * 2,
            transcendentals=0,
        ),
    )(samples, samples, hist, taps, dft)


def fine_kernel(low, own_ref, oth_ref, town_ref, toth_ref, cos_ref, sin_ref, *refs):
    outs, zs = refs[:-1], refs[-1]
    sig, two_c, frames = own_ref.shape
    size = two_c // 2
    r = pl.program_id(0)
    cos, sin = cos_ref[...], sin_ref[...]

    def table(t_ref):
        t = t_ref[...]
        return jnp.concatenate(
            [(t * w).astype(jnp.bfloat16).reshape(frames, LANES) for w in (cos, sin)], axis=1
        )

    acc = jnp.dot(
        own_ref[...].reshape(sig * two_c, frames), table(town_ref), preferred_element_type=jnp.float32
    ) + jnp.dot(
        oth_ref[...].reshape(sig * two_c, frames), table(toth_ref), preferred_element_type=jnp.float32
    )
    acc = acc.reshape(sig, 2, size, 2 * LANES)
    p, q = acc[..., :LANES], acc[..., LANES:]
    pitch = two_c + 1
    real, imag = p[:, 0] + q[:, 1], p[:, 1] - q[:, 0]
    for s in range(sig):
        zs[pl.ds(s * pitch, size), :] = real[s]
        zs[pl.ds(s * pitch + size, size), :] = imag[s]
    for n, out in enumerate(outs):

        @pl.when(r // low == n)
        def _(out=out):
            for c in range(size):
                for part in range(2):
                    out[0, c, part] = zs[pl.ds(part * size + c, sig, stride=pitch), :].astype(
                        jnp.bfloat16
                    )


def fine(own, oth, town, toth, cos, sin, low):
    sig, two_c, frames = own.shape
    dests = cos.shape[0]
    unit = (two_c // 2, 2, sig, LANES)
    highs = dests // low

    def place(n):
        return lambda r: (jnp.clip(r - n * low, 0, low - 1), 0, 0, 0, 0)

    return pl.pallas_call(
        functools.partial(fine_kernel, low),
        grid=(dests,),
        in_specs=[
            pl.BlockSpec(own.shape, lambda r: (0, 0, 0)),
            pl.BlockSpec(oth.shape, lambda r: (0, 0, 0)),
            pl.BlockSpec(town.shape, lambda r: (0, 0, 0)),
            pl.BlockSpec(toth.shape, lambda r: (0, 0, 0)),
            pl.BlockSpec((1,) + cos.shape[1:], lambda r: (r, 0, 0)),
            pl.BlockSpec((1,) + sin.shape[1:], lambda r: (r, 0, 0)),
        ],
        out_specs=[pl.BlockSpec((1,) + unit, place(n)) for n in range(highs)],
        out_shape=[jax.ShapeDtypeStruct((low,) + unit, jnp.bfloat16) for _ in range(highs)],
        scratch_shapes=[pltpu.VMEM((sig * (two_c + 8), LANES), jnp.float32)],
        compiler_params=pltpu.CompilerParams(vmem_limit_bytes=50 << 20),
        cost_estimate=pl.CostEstimate(
            flops=2 * sig * two_c * 2 * frames * dests * 2 * LANES,
            bytes_accessed=6 * sig * two_c * frames,
            transcendentals=0,
        ),
    )(own, oth, town, toth, cos, sin)


def correlate_kernel(sources, scale, per_q, me_ref, *refs):
    ins, out, xr, xi = refs[: len(sources)], refs[-3], refs[-2], refs[-1]
    me = me_ref[0]
    for ref, units in zip(ins, sources):
        for at, rel in units:
            row = pl.multiple_of((me ^ rel) * ROWS, ROWS)
            xr[pl.ds(row, ROWS), :] = ref[at + (0, 0)]
            xi[pl.ds(row, ROWS), :] = ref[at + (0, 1)]
    re, im = xr[...], xi[...]
    lane = lax.broadcasted_iota(jnp.int32, (1, LANES), 1)
    zero = jnp.zeros((), jnp.bfloat16)
    picks = [lane // per_q == q for q in range(LANES // per_q)]
    left = jnp.concatenate(
        [jnp.concatenate([jnp.where(p, re, zero), jnp.where(p, im, zero)], axis=1) for p in picks],
        axis=0,
    )
    dims = (((1,), (1,)), ((), ()))
    for part, right in enumerate((jnp.concatenate([re, im], axis=1), jnp.concatenate([-im, re], axis=1))):
        vis = lax.dot_general(left, right, dims, preferred_element_type=jnp.float32)
        vis = (vis * scale).astype(jnp.bfloat16)
        for q in range(len(picks)):
            out[0, q, part] = vis[q * re.shape[0] : (q + 1) * re.shape[0]]


def correlate_chunk(me, arrays, leads, sources, whole, offset, shape, per_q, scale):
    size = arrays[0].shape[-4]
    signals = shape[-1]
    specs = [pl.BlockSpec(memory_space=pltpu.SMEM)]
    for a, lead in zip(arrays, leads):
        specs.append(
            pl.BlockSpec(
                tuple(lead) + (1,) + a.shape[-3:],
                lambda c, n=len(lead): (0,) * n + (c, 0, 0, 0),
            )
        )
    operands = [me] + list(arrays)
    alias = {}
    if whole is not None:
        alias = {len(operands): 0}
        specs.append(pl.BlockSpec(memory_space=pl.ANY))
        operands.append(whole)
    return pl.pallas_call(
        functools.partial(correlate_kernel, sources, scale, per_q),
        grid=(size,),
        in_specs=specs,
        out_specs=pl.BlockSpec((1,) + shape[1:], lambda c: (c + offset, 0, 0, 0, 0)),
        out_shape=jax.ShapeDtypeStruct(shape, jnp.bfloat16),
        scratch_shapes=[pltpu.VMEM((signals, LANES), jnp.bfloat16)] * 2,
        input_output_aliases=alias,
        compiler_params=pltpu.CompilerParams(vmem_limit_bytes=40 << 20),
        cost_estimate=pl.CostEstimate(
            flops=size * 8 * signals * signals * 4 * LANES,
            bytes_accessed=size * 2 * math.prod(shape[1:]),
            transcendentals=0,
        ),
    )(*operands)


def chunk_sizes(channels):
    eighth = channels // 8
    return [eighth, eighth, 2 * eighth, 2 * eighth, 2 * eighth]


DIRECT = 3


def per_device(samples, coarse_taps, fine_taps):
    sig, samp = samples.shape
    taps_n, frame_len = coarse_taps.shape
    ftaps_n, fine_len = fine_taps.shape
    dests = lax.axis_size("sta")
    me = lax.axis_index("sta")
    win = lax.axis_index("win")
    frames = samp // frame_len
    fine_local = frames // fine_len
    total = fine_local * 2
    per_dest = fine_len // dests
    channels = KEEP // 2
    chunks = chunk_sizes(channels)
    low = 4
    high = dests // low

    hist = from_behind(samples[:, samp - (taps_n - 1) * frame_len :], "win", 1)
    dft = coarse_rows(frame_len, channels, chunks)
    parts = coarse(samples, hist, coarse_taps, dft, chunks)
    own, away = parts[: len(chunks)], parts[len(chunks) :]

    lane = jnp.arange(LANES, dtype=jnp.int32)
    frame_of = lane % total
    weights = fine_taps.astype(jnp.float32)

    def taps_table(side):
        block = side * fine_local + jnp.arange(fine_local, dtype=jnp.int32)
        late = frame_of[None, :] - block[:, None]
        table = jnp.zeros((fine_local, fine_len, LANES), jnp.float32)
        for m in range(ftaps_n):
            table = table + jnp.where((late == m)[:, None, :], weights[m][None, :, None], 0.0)
        return table

    def turn_tables(order):
        fine_of = (me ^ jnp.array(order, jnp.int32))[:, None] * per_dest + (lane // total)[None, :]
        turns = fine_of[:, None, :] * jnp.arange(fine_len, dtype=jnp.int32)[None, :, None]
        angles = (turns % fine_len).astype(jnp.float32) * (2.0 * math.pi / fine_len)
        return jnp.cos(angles), jnp.sin(angles)

    town, toth = taps_table(win), taps_table(1 - win)
    straight = turn_tables(list(range(dests)))
    turned = turn_tables([low * z + 2 * y + c for c in range(2) for y in range(2) for z in range(high)])

    shape = (channels, per_dest, 2, sig * dests, sig * dests)
    result, offset = None, 0
    oths = [swap(away[k], "win", 1) for k in range(len(chunks))]
    for k, size in enumerate(chunks):
        sent = fine(
            own[k], oths[k], town, toth, *(straight if k < DIRECT else turned), low if k < DIRECT else dests // 2
        )
        highs = range(high)
        if k < DIRECT:
            held = [sent[0]] + [swap(sent[n], "sta", low * n) for n in highs if n]
            over = swap(jnp.stack([h[2:] for h in held]), "sta", 2)
            last = swap(jnp.stack([jnp.stack([h[1] for h in held]), over[:, 1]]), "sta", 1)
            arrays = held + [over, last]
            leads = [(1,)] * high + [(high, 1), (2, high)]
            sources = [[((0,), low * n)] for n in highs]
            sources.append([((n, 0), low * n + 2) for n in highs])
            sources.append([((y, n), low * n + 2 * y + 1) for y in range(2) for n in highs])
        else:
            near, pair = sent[0], swap(sent[1], "sta", 1)
            over = swap(jnp.stack([near[high:], pair[high:]]), "sta", 2)
            arrays, leads = [near, pair, over], [(1,), (1,), (2, 1)]
            sources = [[((0,), 0)], [((0,), 1)], [((c, 0), 2 + c) for c in range(2)]]
            for n in highs:
                if n:
                    block = jnp.stack([near[n], pair[n], over[0, n], over[1, n]])
                    arrays.append(swap(block, "sta", low * n))
                    leads.append((low,))
                    sources.append([((b,), low * n + b) for b in range(low)])
        result = correlate_chunk(
            me[None].astype(jnp.int32), arrays, leads, sources, result, offset, shape, total, 1.0 / total
        )
        offset += size
    return result


def serves(mesh, samples, coarse_taps, fine_taps):
    wins, stas = mesh.shape["win"], mesh.shape["sta"]
    sig, samp = samples.shape[0] // stas, samples.shape[1] // wins
    taps_n, frame_len = coarse_taps.shape
    fine_len = fine_taps.shape[1]
    frames = samp // frame_len
    return (
        wins == 2
        and stas % 4 == 0
        and stas & (stas - 1) == 0
        and sig == ROWS
        and taps_n == ROWS
        and frame_len % WIDE == 0
        and frames % BLOCK == 0
        and frames % fine_len == 0
        and fine_len % stas == 0
        and fine_len // stas * (2 * frames // fine_len) == LANES
    )


def solution(mesh):
    placed = (P("sta", "win"), P(), P())

    def step(samples, coarse_taps, fine_taps):
        own_path = serves(mesh, samples, coarse_taps, fine_taps)

        def body(*args):
            if not own_path:
                return per_device_general(*args)
            return per_device(*args)

        f = jax.shard_map(
            body,
            mesh=mesh,
            in_specs=placed,
            out_specs=P("win", "sta", None, None, None),
            check_vma=False,
        )
        return f(samples, coarse_taps, fine_taps)

    return step
```

```python
import functools
import math

import jax
import jax.numpy as jnp
from jax import lax
from jax.experimental import pallas as pl
from jax.experimental.pallas import tpu as pltpu
from jax.sharding import PartitionSpec as P

KEEP = 128
LANES = 128
WIDE = 256
PITCH = 17
GROUP = 4
VMEM = 63 << 20
ROWS = 16
BLOCK = 128


def from_behind(x, axis, by):
    size = lax.axis_size(axis)
    pairs = [(i, i + by) for i in range(size) if 0 <= i + by < size]
    return lax.ppermute(x, axis, pairs)


def coarse_matrix(frame_len, band_count):
    channels = frame_len // 8 + jnp.arange(band_count, dtype=jnp.int32)
    products = jnp.arange(frame_len, dtype=jnp.int32)[:, None] * channels[None, :]
    angles = (products % frame_len).astype(jnp.float32) * (2.0 * math.pi / frame_len)
    return jnp.concatenate([jnp.cos(angles), -jnp.sin(angles)], axis=1).astype(jnp.bfloat16)


def fine_tables(fine_len):
    products = (
        jnp.arange(fine_len, dtype=jnp.int32)[:, None]
        * jnp.arange(fine_len, dtype=jnp.int32)[None, :]
    )
    angles = (products % fine_len).astype(jnp.float32) * (2.0 * math.pi / fine_len)
    return (jnp.cos(angles), jnp.sin(angles))


def correlate(spectra_in, pieces):
    band_local, fine_local, sig_count, columns = spectra_in.shape
    split_view = spectra_in.reshape(
        band_local, fine_local, sig_count, pieces, 2, columns // (2 * pieces)
    )
    turned = jnp.stack([split_view[:, :, :, :, 1], -split_view[:, :, :, :, 0]], axis=4).reshape(
        band_local, fine_local, sig_count, columns
    )
    real_vis = jnp.einsum(
        "kqsc,kqtc->kqst", spectra_in, spectra_in, preferred_element_type=jnp.float32
    )
    imag_vis = jnp.einsum("kqsc,kqtc->kqst", turned, spectra_in, preferred_element_type=jnp.float32)
    return jnp.stack([real_vis, imag_vis], axis=2)


def per_device_general(samples, coarse_taps, fine_taps):
    sig_local, samp_local = samples.shape
    tap_count, frame_len = coarse_taps.shape
    fine_tap_count, fine_len = fine_taps.shape
    band_count = KEEP
    frame_count = samp_local // frame_len
    frames_local = samples.reshape(sig_local, frame_count, frame_len)
    earlier = from_behind(frames_local[:, frame_count - (tap_count - 1) :], "win", 1)
    padded = jnp.concatenate([earlier, frames_local], axis=1)
    windowed = jnp.zeros((sig_local, frame_count, frame_len), jnp.float32)
    for tap_index in range(tap_count):
        start = tap_count - 1 - tap_index
        windowed = windowed + coarse_taps[tap_index].astype(jnp.float32)[None, None, :] * padded[
            :, start : start + frame_count
        ].astype(jnp.float32)
    spectra = jnp.dot(
        windowed.astype(jnp.bfloat16).reshape(sig_local * frame_count, frame_len),
        coarse_matrix(frame_len, band_count),
        preferred_element_type=jnp.float32,
    )
    spectra = spectra.astype(jnp.bfloat16).reshape(sig_local, frame_count, 2 * band_count)
    history = (fine_tap_count - 1) * fine_len
    carried = from_behind(spectra[:, frame_count - history :], "win", 1)
    extended = jnp.concatenate([carried, spectra], axis=1)
    fine_count = frame_count // fine_len
    groups = extended.reshape(sig_local, fine_count + fine_tap_count - 1, fine_len, 2, band_count)
    filtered = jnp.zeros((sig_local, fine_count, fine_len, 2, band_count), jnp.float32)
    for tap_index in range(fine_tap_count):
        start = fine_tap_count - 1 - tap_index
        filtered = filtered + fine_taps[tap_index].astype(jnp.float32)[
            None, None, :, None, None
        ] * groups[:, start : start + fine_count].astype(jnp.float32)
    cosines, sines = fine_tables(fine_len)
    real_part = filtered[:, :, :, 0]
    imag_part = filtered[:, :, :, 1]
    highest = lax.Precision.HIGHEST
    out_real = jnp.einsum("qj,sgjk->kqsg", cosines, real_part, precision=highest) + jnp.einsum(
        "qj,sgjk->kqsg", sines, imag_part, precision=highest
    )
    out_imag = jnp.einsum("qj,sgjk->kqsg", cosines, imag_part, precision=highest) - jnp.einsum(
        "qj,sgjk->kqsg", sines, real_part, precision=highest
    )
    local_spectra = (
        jnp.stack([out_real, out_imag], axis=3)
        .astype(jnp.bfloat16)
        .reshape(band_count, fine_len, sig_local, 2 * fine_count)
    )
    frame_total = fine_count * lax.axis_size("win")
    moved = lax.all_to_all(local_spectra, "sta", split_axis=1, concat_axis=2, tiled=True)
    moved = lax.all_to_all(moved, "win", split_axis=0, concat_axis=3, tiled=True)
    vis_local = correlate(moved, lax.axis_size("win"))
    return (vis_local / frame_total).astype(jnp.bfloat16)


def swap(x, axis, by):
    return lax.ppermute(x, axis, [(i, i ^ by) for i in range(lax.axis_size(axis))])


def coarse_rows(frame_len, band_half, chunks):
    half = lax.axis_index("win")
    rows = []
    for h in range(2):
        base = 0
        for size in chunks:
            for part in range(2):
                channel = (half ^ h) * band_half + base + jnp.arange(size, dtype=jnp.int32)
                rows.append(channel * 2 + part)
            base += size
    code = jnp.concatenate(rows)
    channel = frame_len // 8 + code // 2
    products = channel[:, None] * jnp.arange(frame_len, dtype=jnp.int32)[None, :]
    angles = (products % frame_len).astype(jnp.float32) * (2.0 * math.pi / frame_len)
    return jnp.where((code % 2 == 0)[:, None], jnp.cos(angles), -jnp.sin(angles)).astype(jnp.bfloat16)


def coarse_kernel(chunks, taps_n, x_ref, before_ref, hist_ref, taps_ref, dft_ref, *refs):
    outs, (xs, even, odd) = refs[:-3], refs[-3:]
    step, last = pl.program_id(0), pl.num_programs(0) - 1
    keep = taps_n - 1
    pieces = xs.shape[1]
    skip = before_ref.shape[1] // (pieces * WIDE) - keep
    group = 8

    def load():
        @pl.when(step == 0)
        def _():
            for f in range(keep):
                for j in range(pieces):
                    at = (f * pieces + j) * WIDE
                    xs[f, j] = hist_ref[:, at : at + WIDE]

        @pl.when(step > 0)
        def _():
            for f in range(keep):
                for j in range(pieces):
                    at = ((f + skip) * pieces + j) * WIDE
                    xs[f, j] = before_ref[:, at : at + WIDE]

        def move(f, _):
            for j in range(pieces):
                at = pl.multiple_of((f * pieces + j) * WIDE, WIDE)
                xs[keep + f, j] = x_ref[:, pl.ds(at, WIDE)]
            return 0

        lax.fori_loop(0, BLOCK, move, 0, unroll=8)

    def fir(wd, first, j):
        taps = [taps_ref[j, m] for m in range(taps_n)]
        xv = [xs[first + t, j] for t in range(group + keep)]
        for g in range(group):
            terms = [taps[m] * xv[g + keep - m] for m in range(taps_n)]
            for _ in range(1):
                terms = [a + b for a, b in zip(terms[::2], terms[1::2])]
            wide = [t.astype(jnp.float32) for t in terms]
            while len(wide) > 1:
                wide = [a + b for a, b in zip(wide[::2], wide[1::2])]
            rows = pl.ds((first + g) * PITCH, ROWS)
            for n in range(WIDE // LANES):
                wd[j * (WIDE // LANES) + n, rows, :] = wide[0][:, n * LANES : (n + 1) * LANES]

    def project(wd, p):
        rows = []
        for t in range(2):
            parts = [wd[j, pl.ds(2 * p + t, BLOCK, stride=PITCH), :] for j in range(wd.shape[0])]
            rows.append(jnp.concatenate(parts, axis=1).astype(jnp.bfloat16))
        both = jnp.concatenate(rows, axis=0)
        res = lax.dot_general(
            dft_ref[...], both, (((1,), (1,)), ((), ())), preferred_element_type=jnp.float32
        ).astype(jnp.bfloat16)
        for t in range(2):
            base = 0
            for n, out in enumerate(outs):
                size = 2 * chunks[n % len(chunks)]
                out[2 * p + t] = res[base : base + size, t * BLOCK : (t + 1) * BLOCK]
                base += size

    pairs = ROWS // 2
    share = BLOCK // pairs // group

    def run(fill, drain):
        def body(p, _):
            if drain is not None:
                project(drain, p)
            if fill is not None:
                for n in range(share):
                    for j in range(pieces):
                        fir(fill, (p * share + n) * group, j)
            return 0

        if fill is not None:
            load()
        lax.fori_loop(0, pairs, body, 0)

    @pl.when(step == 0)
    def _():
        run(even, None)

    @pl.when((step > 0) & (step < last) & (step % 2 == 1))
    def _():
        run(odd, even)

    @pl.when((step > 0) & (step < last) & (step % 2 == 0))
    def _():
        run(even, odd)

    @pl.when((step == last) & (step % 2 == 1))
    def _():
        run(None, even)

    @pl.when((step == last) & (step % 2 == 0))
    def _():
        run(None, odd)


def coarse(samples, hist, coarse_taps, dft, chunks):
    sig, samp = samples.shape
    taps_n, frame_len = coarse_taps.shape
    pieces = frame_len // WIDE
    frames = samp // frame_len
    before = taps_n
    taps = jnp.broadcast_to(
        coarse_taps.reshape(taps_n, pieces, WIDE).transpose(1, 0, 2)[:, :, None],
        (pieces, taps_n, ROWS, WIDE),
    )
    ratio = BLOCK // before
    blocks = frames // BLOCK
    shapes = [jax.ShapeDtypeStruct((sig, 2 * c, frames), jnp.bfloat16) for c in chunks * 2]

    def at(i):
        return jnp.minimum(i, blocks - 1)

    return pl.pallas_call(
        functools.partial(coarse_kernel, chunks, taps_n),
        grid=(blocks + 1,),
        in_specs=[
            pl.BlockSpec((sig, BLOCK * frame_len), lambda i: (0, at(i))),
            pl.BlockSpec((sig, before * frame_len), lambda i: (0, jnp.maximum(at(i) * ratio - 1, 0))),
            pl.BlockSpec(hist.shape, lambda i: (0, 0)),
            pl.BlockSpec(taps.shape, lambda i: (0, 0, 0, 0)),
            pl.BlockSpec(dft.shape, lambda i: (0, 0)),
        ],
        out_specs=[
            pl.BlockSpec((sig, 2 * c, BLOCK), lambda i: (0, 0, jnp.maximum(i - 1, 0)))
            for c in chunks * 2
        ],
        out_shape=shapes,
        scratch_shapes=[pltpu.VMEM((BLOCK + taps_n - 1, pieces, sig, WIDE), jnp.bfloat16)]
        + [pltpu.VMEM((frame_len // LANES, BLOCK * PITCH, LANES), jnp.float32)] * 2,
        compiler_params=pltpu.CompilerParams(vmem_limit_bytes=VMEM),
        cost_estimate=pl.CostEstimate(
            flops=2 * sig * frames * frame_len * (dft.shape[0] + 128 * taps_n),
            bytes_accessed=2 * sig * samp * 2,
            transcendentals=0,
        ),
    )(samples, samples, hist, taps, dft)


def fill_tables(tables, town_ref, toth_ref, cos_ref, sin_ref, u):
    fine_local, fine_len, _ = town_ref.shape
    frames = fine_local * fine_len
    for side, t_ref in enumerate((town_ref, toth_ref)):
        for part, turn in enumerate((cos_ref[u], sin_ref[u])):
            rows = (t_ref[...] * turn).astype(jnp.bfloat16).reshape(frames, LANES)
            tables[u, side * frames : (side + 1) * frames, part * LANES : (part + 1) * LANES] = rows


def fine_kernel(steps, first, own_ref, oth_ref, *refs):
    if first:
        makers, outs, table_ref, zs = refs[:4], refs[4:-2], refs[-2], refs[-1]
    else:
        table_ref, outs, zs = refs[0], refs[1:-1], refs[-1]
    sig, two_c, frames = own_ref.shape
    size = two_c // 2
    pitch = two_c + 1
    step = pl.program_id(0)
    units = table_ref.shape[0] * table_ref.shape[1]
    span = sig * (two_c + 8)
    tables = table_ref.reshape(units, 2 * frames, 2 * LANES)
    for u in range(units):
        if first:
            fill_tables(tables, *makers, u)
        acc = jnp.dot(
            own_ref[...].reshape(sig * two_c, frames),
            tables[u, :frames],
            preferred_element_type=jnp.float32,
        ) + jnp.dot(
            oth_ref[...].reshape(sig * two_c, frames),
            tables[u, frames:],
            preferred_element_type=jnp.float32,
        )
        acc = acc.reshape(sig, 2, size, 2 * LANES)
        p, q = acc[..., :LANES], acc[..., LANES:]
        real, imag = p[:, 0] + q[:, 1], p[:, 1] - q[:, 0]
        for s in range(sig):
            zs[pl.ds(u * span + s * pitch, size), :] = real[s]
            zs[pl.ds(u * span + s * pitch + size, size), :] = imag[s]
    for n, out in enumerate(outs):

        @pl.when(step // steps == n)
        def _(out=out):
            for u in range(units):
                for c in range(size):
                    for part in range(2):
                        at = pl.ds(u * span + part * size + c, sig, stride=pitch)
                        out[u, c, part] = zs[at, :].astype(jnp.bfloat16)


def fine(own, oth, tables, turned, makers=None):
    sig, two_c, frames = own.shape
    first = makers is not None
    if first:
        dests = makers[2].shape[0]
        tables = jax.ShapeDtypeStruct((dests // 4, 4, 2 * frames, 2 * LANES), jnp.bfloat16)
    high, low = tables.shape[:2]
    unit = (two_c // 2, 2, sig, LANES)
    if turned:
        grid, units, count = low, high, 2
        spec = pl.BlockSpec((high, 1) + tables.shape[2:], lambda t: (0, t % 2 * 2 + t // 2, 0, 0))
    else:
        grid, units, count = high, low, high
        spec = pl.BlockSpec((1, low) + tables.shape[2:], lambda t: (t, 0, 0, 0))
    steps = grid // count

    def place(n):
        return lambda t: (jnp.clip(t - n * steps, 0, steps - 1), 0, 0, 0, 0)

    whole = pl.BlockSpec(own.shape, lambda t: (0, 0, 0))
    out_specs = [pl.BlockSpec((units,) + unit, place(n)) for n in range(count)]
    out_shape = [jax.ShapeDtypeStruct((steps * units,) + unit, jnp.bfloat16) for _ in range(count)]
    if first:
        kept = pl.BlockSpec(makers[0].shape, lambda t: (0, 0, 0))
        turn = pl.BlockSpec((low,) + makers[2].shape[1:], lambda t: (t, 0, 0))
        in_specs, operands = [whole, whole, kept, kept, turn, turn], (own, oth, *makers)
        out_specs, out_shape = out_specs + [spec], out_shape + [tables]
    else:
        in_specs, operands = [whole, whole, spec], (own, oth, tables)
    return pl.pallas_call(
        functools.partial(fine_kernel, steps, first),
        grid=(grid,),
        in_specs=in_specs,
        out_specs=out_specs,
        out_shape=out_shape,
        scratch_shapes=[pltpu.VMEM((units * sig * (two_c + 8), LANES), jnp.float32)],
        compiler_params=pltpu.CompilerParams(vmem_limit_bytes=VMEM),
        cost_estimate=pl.CostEstimate(
            flops=2 * sig * two_c * 2 * frames * high * low * 2 * LANES,
            bytes_accessed=6 * sig * two_c * frames + 8 * high * low * frames * LANES,
            transcendentals=0,
        ),
    )(*operands)


def pack_kernel(*refs):
    ins, out = refs[:-1], refs[-1]
    for n, ref in enumerate(ins):
        out[n] = ref[(0,) * (len(ref.shape) - 4)]


def pack(slots):
    size = slots[0][0].shape[-4]
    tail = slots[0][0].shape[-3:]
    half = size // 2
    return pl.pallas_call(
        pack_kernel,
        grid=(2,),
        in_specs=[
            pl.BlockSpec((1,) * len(at) + (half,) + tail, lambda c, at=at: at + (c, 0, 0, 0))
            for _, at in slots
        ],
        out_specs=pl.BlockSpec((len(slots), half) + tail, lambda c: (0, c, 0, 0, 0)),
        out_shape=jax.ShapeDtypeStruct((len(slots), size) + tail, jnp.bfloat16),
        compiler_params=pltpu.CompilerParams(vmem_limit_bytes=VMEM),
        cost_estimate=pl.CostEstimate(
            flops=0, bytes_accessed=4 * len(slots) * size * math.prod(tail), transcendentals=0
        ),
    )(*[array for array, _ in slots])


def correlate_kernel(sources, scale, per_q, me_ref, *refs):
    ins, out, xr, xi = refs[: len(sources)], refs[-3], refs[-2], refs[-1]
    me = me_ref[0]
    for ref, units in zip(ins, sources):
        for at, rel in units:
            row = pl.ds(pl.multiple_of((me ^ rel) * ROWS, ROWS), ROWS)
            for c in range(out.shape[0]):
                xr[c, row, :] = ref[at + (c, 0)]
                xi[c, row, :] = ref[at + (c, 1)]
    lane = lax.broadcasted_iota(jnp.int32, (1, LANES), 1)
    zero = jnp.zeros((), jnp.bfloat16)
    picks = [lane // per_q == q for q in range(LANES // per_q)]
    dims = (((1,), (1,)), ((), ()))

    def body(c, _):
        re, im = xr[c], xi[c]
        for part in range(2):
            right = jnp.concatenate([-im, re] if part else [re, im], axis=1)
            for q, pick in enumerate(picks):
                left = jnp.concatenate([jnp.where(pick, re, zero), jnp.where(pick, im, zero)], axis=1)
                vis = lax.dot_general(left, right, dims, preferred_element_type=jnp.float32)
                out[c, q, part] = (vis * scale).astype(jnp.bfloat16)
        return 0

    lax.fori_loop(0, out.shape[0], body, 0)


def correlate_chunk(me, arrays, leads, sources, whole, offset, shape, per_q, scale):
    size = arrays[0].shape[-4]
    signals = shape[-1]
    specs = [pl.BlockSpec(memory_space=pltpu.SMEM)]
    for a, lead in zip(arrays, leads):
        specs.append(
            pl.BlockSpec(
                tuple(lead) + (GROUP,) + a.shape[-3:],
                lambda c, n=len(lead): (0,) * n + (c, 0, 0, 0),
            )
        )
    operands = [me] + list(arrays)
    alias = {}
    if whole is not None:
        alias = {len(operands): 0}
        specs.append(pl.BlockSpec(memory_space=pl.ANY))
        operands.append(whole)
    return pl.pallas_call(
        functools.partial(correlate_kernel, sources, scale, per_q),
        grid=(size // GROUP,),
        in_specs=specs,
        out_specs=pl.BlockSpec((GROUP,) + shape[1:], lambda c: (c + offset // GROUP, 0, 0, 0, 0)),
        out_shape=jax.ShapeDtypeStruct(shape, jnp.bfloat16),
        scratch_shapes=[pltpu.VMEM((GROUP, signals, LANES), jnp.bfloat16)] * 2,
        input_output_aliases=alias,
        compiler_params=pltpu.CompilerParams(vmem_limit_bytes=VMEM),
        cost_estimate=pl.CostEstimate(
            flops=size * 8 * signals * signals * 4 * LANES,
            bytes_accessed=size * 2 * math.prod(shape[1:]),
            transcendentals=0,
        ),
    )(*operands)


def chunk_sizes(channels):
    eighth = channels // 8
    return [eighth, 2 * eighth, 2 * eighth, 2 * eighth, eighth]


DIRECT = 2


def per_device(samples, coarse_taps, fine_taps):
    sig, samp = samples.shape
    taps_n, frame_len = coarse_taps.shape
    ftaps_n, fine_len = fine_taps.shape
    dests = lax.axis_size("sta")
    me = lax.axis_index("sta")
    win = lax.axis_index("win")
    frames = samp // frame_len
    fine_local = frames // fine_len
    total = fine_local * 2
    per_dest = fine_len // dests
    channels = KEEP // 2
    chunks = chunk_sizes(channels)
    low = 4
    high = dests // low

    hist = from_behind(samples[:, samp - (taps_n - 1) * frame_len :], "win", 1)
    dft = coarse_rows(frame_len, channels, chunks)
    parts = coarse(samples, hist, coarse_taps, dft, chunks)
    own, away = parts[: len(chunks)], parts[len(chunks) :]

    lane = jnp.arange(LANES, dtype=jnp.int32)
    frame_of = lane % total
    weights = fine_taps.astype(jnp.float32)

    def taps_table(side):
        block = side * fine_local + jnp.arange(fine_local, dtype=jnp.int32)
        late = frame_of[None, :] - block[:, None]
        table = jnp.zeros((fine_local, fine_len, LANES), jnp.float32)
        for m in range(ftaps_n):
            table = table + jnp.where((late == m)[:, None, :], weights[m][None, :, None], 0.0)
        return table

    fine_of = (me ^ jnp.arange(dests, dtype=jnp.int32))[:, None] * per_dest + (lane // total)[None, :]
    turns = fine_of[:, None, :] * jnp.arange(fine_len, dtype=jnp.int32)[None, :, None]
    angles = (turns % fine_len).astype(jnp.float32) * (2.0 * math.pi / fine_len)
    makers = (taps_table(win), taps_table(1 - win), jnp.cos(angles), jnp.sin(angles))

    shape = (channels, per_dest, 2, sig * dests, sig * dests)
    highs = range(high)
    oths = [swap(away[k], "win", 1) for k in range(len(chunks))]

    pieces = []
    for k in range(len(chunks)):
        if k == 0:
            *sent, tables = fine(own[k], oths[k], None, False, makers)
        else:
            sent = fine(own[k], oths[k], tables, k >= DIRECT)
        if k < DIRECT:
            held = [sent[0]] + [swap(sent[n], "sta", low * n) for n in highs if n]
            block = pack([(h, (2 + c,)) for c in range(2) for h in held])
            over = swap(block, "sta", 2)
            block = pack([(h, (1,)) for h in held] + [(over, (high + n,)) for n in highs])
            last = swap(block, "sta", 1)
            arrays = held + [over, last]
            leads = [(1,)] * high + [(high,), (2 * high,)]
            sources = [[((0,), low * n)] for n in highs]
            sources.append([((n,), low * n + 2) for n in highs])
            sources.append([((y * high + n,), low * n + 2 * y + 1) for y in range(2) for n in highs])
        else:
            near, pair = sent[0], swap(sent[1], "sta", 1)
            block = pack([(a, (high + n,)) for n in highs for a in (near, pair)])
            over = swap(block, "sta", 2)
            arrays, leads = [near, pair, over], [(1,), (1,), (2,)]
            sources = [[((0,), 0)], [((0,), 1)], [((c,), 2 + c) for c in range(2)]]
            for n in highs:
                if n:
                    slots = [(near, (n,)), (pair, (n,)), (over, (2 * n,)), (over, (2 * n + 1,))]
                    block = pack(slots)
                    arrays.append(swap(block, "sta", low * n))
                    leads.append((low,))
                    sources.append([((b,), low * n + b) for b in range(low)])
        pieces.append((arrays, leads, sources))
    result = None
    who = me[None].astype(jnp.int32)
    for k in range(len(chunks)):
        result = correlate_chunk(
            who, *pieces[k], result, sum(chunks[:k]), shape, total, 1.0 / total
        )
    return result


def serves(mesh, samples, coarse_taps, fine_taps):
    wins, stas = mesh.shape["win"], mesh.shape["sta"]
    sig, samp = samples.shape[0] // stas, samples.shape[1] // wins
    taps_n, frame_len = coarse_taps.shape
    fine_len = fine_taps.shape[1]
    frames = samp // frame_len
    return (
        wins == 2
        and stas % 4 == 0
        and stas & (stas - 1) == 0
        and sig == ROWS
        and taps_n == ROWS
        and frame_len % WIDE == 0
        and frames % BLOCK == 0
        and frames % fine_len == 0
        and fine_len % stas == 0
        and fine_len // stas * (2 * frames // fine_len) == LANES
    )


def solution(mesh):
    placed = (P("sta", "win"), P(), P())

    def step(samples, coarse_taps, fine_taps):
        own_path = serves(mesh, samples, coarse_taps, fine_taps)

        def body(*args):
            if not own_path:
                return per_device_general(*args)
            return per_device(*args)

        f = jax.shard_map(
            body,
            mesh=mesh,
            in_specs=placed,
            out_specs=P("win", "sta", None, None, None),
            check_vma=False,
        )
        return f(samples, coarse_taps, fine_taps)

    return step
```

```python
import functools
import math

import jax
import jax.numpy as jnp
import numpy as np
from jax import lax
from jax.experimental import pallas as pl
from jax.experimental.pallas import tpu as pltpu
from jax.sharding import PartitionSpec as P

KEEP = 128
LANES = 128
WIDE = 256
PITCH = 17
GROUP = 4
VMEM = 63 << 20
ROWS = 16
BLOCK = 128


def from_behind(x, axis, by):
    size = lax.axis_size(axis)
    pairs = [(i, i + by) for i in range(size) if 0 <= i + by < size]
    return lax.ppermute(x, axis, pairs)


def coarse_matrix(frame_len, band_count):
    channels = frame_len // 8 + jnp.arange(band_count, dtype=jnp.int32)
    products = jnp.arange(frame_len, dtype=jnp.int32)[:, None] * channels[None, :]
    angles = (products % frame_len).astype(jnp.float32) * (2.0 * math.pi / frame_len)
    return jnp.concatenate([jnp.cos(angles), -jnp.sin(angles)], axis=1).astype(jnp.bfloat16)


def fine_tables(fine_len):
    products = (
        jnp.arange(fine_len, dtype=jnp.int32)[:, None]
        * jnp.arange(fine_len, dtype=jnp.int32)[None, :]
    )
    angles = (products % fine_len).astype(jnp.float32) * (2.0 * math.pi / fine_len)
    return (jnp.cos(angles), jnp.sin(angles))


def correlate(spectra_in, pieces):
    band_local, fine_local, sig_count, columns = spectra_in.shape
    split_view = spectra_in.reshape(
        band_local, fine_local, sig_count, pieces, 2, columns // (2 * pieces)
    )
    turned = jnp.stack([split_view[:, :, :, :, 1], -split_view[:, :, :, :, 0]], axis=4).reshape(
        band_local, fine_local, sig_count, columns
    )
    real_vis = jnp.einsum(
        "kqsc,kqtc->kqst", spectra_in, spectra_in, preferred_element_type=jnp.float32
    )
    imag_vis = jnp.einsum("kqsc,kqtc->kqst", turned, spectra_in, preferred_element_type=jnp.float32)
    return jnp.stack([real_vis, imag_vis], axis=2)


def per_device_general(samples, coarse_taps, fine_taps):
    sig_local, samp_local = samples.shape
    tap_count, frame_len = coarse_taps.shape
    fine_tap_count, fine_len = fine_taps.shape
    band_count = KEEP
    frame_count = samp_local // frame_len
    frames_local = samples.reshape(sig_local, frame_count, frame_len)
    earlier = from_behind(frames_local[:, frame_count - (tap_count - 1) :], "win", 1)
    padded = jnp.concatenate([earlier, frames_local], axis=1)
    windowed = jnp.zeros((sig_local, frame_count, frame_len), jnp.float32)
    for tap_index in range(tap_count):
        start = tap_count - 1 - tap_index
        windowed = windowed + coarse_taps[tap_index].astype(jnp.float32)[None, None, :] * padded[
            :, start : start + frame_count
        ].astype(jnp.float32)
    spectra = jnp.dot(
        windowed.astype(jnp.bfloat16).reshape(sig_local * frame_count, frame_len),
        coarse_matrix(frame_len, band_count),
        preferred_element_type=jnp.float32,
    )
    spectra = spectra.astype(jnp.bfloat16).reshape(sig_local, frame_count, 2 * band_count)
    history = (fine_tap_count - 1) * fine_len
    carried = from_behind(spectra[:, frame_count - history :], "win", 1)
    extended = jnp.concatenate([carried, spectra], axis=1)
    fine_count = frame_count // fine_len
    groups = extended.reshape(sig_local, fine_count + fine_tap_count - 1, fine_len, 2, band_count)
    filtered = jnp.zeros((sig_local, fine_count, fine_len, 2, band_count), jnp.float32)
    for tap_index in range(fine_tap_count):
        start = fine_tap_count - 1 - tap_index
        filtered = filtered + fine_taps[tap_index].astype(jnp.float32)[
            None, None, :, None, None
        ] * groups[:, start : start + fine_count].astype(jnp.float32)
    cosines, sines = fine_tables(fine_len)
    real_part = filtered[:, :, :, 0]
    imag_part = filtered[:, :, :, 1]
    highest = lax.Precision.HIGHEST
    out_real = jnp.einsum("qj,sgjk->kqsg", cosines, real_part, precision=highest) + jnp.einsum(
        "qj,sgjk->kqsg", sines, imag_part, precision=highest
    )
    out_imag = jnp.einsum("qj,sgjk->kqsg", cosines, imag_part, precision=highest) - jnp.einsum(
        "qj,sgjk->kqsg", sines, real_part, precision=highest
    )
    local_spectra = (
        jnp.stack([out_real, out_imag], axis=3)
        .astype(jnp.bfloat16)
        .reshape(band_count, fine_len, sig_local, 2 * fine_count)
    )
    frame_total = fine_count * lax.axis_size("win")
    moved = lax.all_to_all(local_spectra, "sta", split_axis=1, concat_axis=2, tiled=True)
    moved = lax.all_to_all(moved, "win", split_axis=0, concat_axis=3, tiled=True)
    vis_local = correlate(moved, lax.axis_size("win"))
    return (vis_local / frame_total).astype(jnp.bfloat16)


def swap(x, axis, by):
    return lax.ppermute(x, axis, [(i, i ^ by) for i in range(lax.axis_size(axis))])


def coarse_rows(frame_len, band_half, chunks):
    rows = []
    for h in range(2):
        base = frame_len // 8 + h * band_half
        for size in chunks:
            channel = np.arange(base, base + size, dtype=np.int32)
            products = channel[:, None] * np.arange(frame_len, dtype=np.int32)[None, :]
            angles = (products % frame_len).astype(np.float32) * np.float32(2.0 * math.pi / frame_len)
            rows += [np.cos(angles), -np.sin(angles)]
            base += size
    return np.concatenate(rows).reshape(2, 2 * band_half, frame_len).astype(jnp.bfloat16)


def coarse_kernel(chunks, taps_n, win_ref, x_ref, before_ref, taps_ref, dft_ref, *refs):
    opening = len(refs) > 3 + 2 * len(chunks)
    hist_ref, refs = (refs[0], refs[1:]) if opening else (None, refs)
    outs, (xs, even, odd) = refs[:-3], refs[-3:]
    step, last = pl.program_id(0), pl.num_programs(0) - 1
    keep = taps_n - 1
    pieces = xs.shape[1]
    skip = before_ref.shape[1] // (pieces * WIDE) - keep
    group = 8

    def load():
        def put(ref, gap):
            for f in range(keep):
                for j in range(pieces):
                    at = ((f + gap) * pieces + j) * WIDE
                    xs[f, j] = ref[:, at : at + WIDE]

        if opening:
            pl.when(step == 0)(lambda: put(hist_ref, 0))
            pl.when(step > 0)(lambda: put(before_ref, skip))
        else:
            put(before_ref, skip)

        def move(f, _):
            for j in range(pieces):
                at = pl.multiple_of((f * pieces + j) * WIDE, WIDE)
                xs[keep + f, j] = x_ref[:, pl.ds(at, WIDE)]
            return 0

        lax.fori_loop(0, BLOCK, move, 0, unroll=8)

    def fir(wd, first, j):
        taps = [taps_ref[j, m] for m in range(taps_n)]
        xv = [xs[first + t, j] for t in range(group + keep)]
        for g in range(group):
            terms = [taps[m] * xv[g + keep - m] for m in range(taps_n)]
            for _ in range(2):
                terms = [a + b for a, b in zip(terms[::2], terms[1::2])]
            wide = [t.astype(jnp.float32) for t in terms]
            while len(wide) > 1:
                wide = [a + b for a, b in zip(wide[::2], wide[1::2])]
            rows = pl.ds((first + g) * PITCH, ROWS)
            for n in range(WIDE // LANES):
                wd[j * (WIDE // LANES) + n, rows, :] = wide[0][:, n * LANES : (n + 1) * LANES]

    def project(wd, p):
        rows = []
        for t in range(2):
            parts = [wd[j, pl.ds(2 * p + t, BLOCK, stride=PITCH), :] for j in range(wd.shape[0])]
            rows.append(jnp.concatenate(parts, axis=1).astype(jnp.bfloat16))
        both = jnp.concatenate(rows, axis=0)
        mine = win_ref[0]
        matrix = jnp.concatenate([dft_ref[mine], dft_ref[1 - mine]], axis=0)
        res = lax.dot_general(
            matrix, both, (((1,), (1,)), ((), ())), preferred_element_type=jnp.float32
        ).astype(jnp.bfloat16)
        for t in range(2):
            base = 0
            for n, out in enumerate(outs):
                size = 2 * chunks[n % len(chunks)]
                out[2 * p + t] = res[base : base + size, t * BLOCK : (t + 1) * BLOCK]
                base += size

    pairs = ROWS // 2
    share = BLOCK // pairs // group

    def run(fill, drain):
        def body(p, _):
            if drain is not None:
                project(drain, p)
            if fill is not None:
                for n in range(share):
                    for j in range(pieces):
                        fir(fill, (p * share + n) * group, j)
            return 0

        if fill is not None:
            load()
        lax.fori_loop(0, pairs, body, 0)

    @pl.when(step == 0)
    def _():
        run(even, None)

    @pl.when((step > 0) & (step < last) & (step % 2 == 1))
    def _():
        run(odd, even)

    @pl.when((step > 0) & (step < last) & (step % 2 == 0))
    def _():
        run(even, odd)

    @pl.when((step == last) & (step % 2 == 1))
    def _():
        run(None, even)

    @pl.when((step == last) & (step % 2 == 0))
    def _():
        run(None, odd)


def coarse(win, samples, hist, coarse_taps, dft, chunks, start, blocks):
    sig, _ = samples.shape
    taps_n, frame_len = coarse_taps.shape
    pieces = frame_len // WIDE
    frames = blocks * BLOCK
    before = taps_n
    taps = jnp.broadcast_to(
        coarse_taps.reshape(taps_n, pieces, WIDE).transpose(1, 0, 2)[:, :, None],
        (pieces, taps_n, ROWS, WIDE),
    )
    ratio = BLOCK // before
    shapes = [jax.ShapeDtypeStruct((sig, 2 * c, frames), jnp.bfloat16) for c in chunks * 2]

    def at(i):
        return start + jnp.minimum(i, blocks - 1)

    return pl.pallas_call(
        functools.partial(coarse_kernel, chunks, taps_n),
        grid=(blocks + 1,),
        in_specs=[
            pl.BlockSpec(memory_space=pltpu.SMEM),
            pl.BlockSpec((sig, BLOCK * frame_len), lambda i: (0, at(i))),
            pl.BlockSpec((sig, before * frame_len), lambda i: (0, jnp.maximum(at(i) * ratio - 1, 0))),
            pl.BlockSpec(taps.shape, lambda i: (0, 0, 0, 0)),
            pl.BlockSpec(dft.shape, lambda i: (0, 0, 0)),
        ]
        + [pl.BlockSpec(h.shape, lambda i: (0, 0)) for h in hist],
        out_specs=[
            pl.BlockSpec((sig, 2 * c, BLOCK), lambda i: (0, 0, jnp.maximum(i - 1, 0)))
            for c in chunks * 2
        ],
        out_shape=shapes,
        scratch_shapes=[pltpu.VMEM((BLOCK + taps_n - 1, pieces, sig, WIDE), jnp.bfloat16)]
        + [pltpu.VMEM((frame_len // LANES, BLOCK * PITCH, LANES), jnp.float32)] * 2,
        compiler_params=pltpu.CompilerParams(vmem_limit_bytes=VMEM),
        cost_estimate=pl.CostEstimate(
            flops=2 * sig * frames * frame_len * (dft.shape[0] * dft.shape[1] + 128 * taps_n),
            bytes_accessed=4 * sig * frames * frame_len,
            transcendentals=0,
        ),
    )(win, samples, samples, taps, dft, *hist)


def fill_tables(tables, town_ref, toth_ref, cos_ref, sin_ref, u):
    fine_local, fine_len, _ = town_ref.shape
    frames = fine_local * fine_len
    for side, t_ref in enumerate((town_ref, toth_ref)):
        for part, turn in enumerate((cos_ref[u], sin_ref[u])):
            rows = (t_ref[...] * turn).astype(jnp.bfloat16).reshape(frames, LANES)
            tables[u, side * frames : (side + 1) * frames, part * LANES : (part + 1) * LANES] = rows


def fine_kernel(steps, first, count, *refs):
    parts, refs = refs[:count], refs[count:]
    if first:
        makers, outs, table_ref, zs = refs[:4], refs[4:-2], refs[-2], refs[-1]
    else:
        table_ref, outs, zs = refs[0], refs[1:-1], refs[-1]
    sig, two_c, frames = parts[0].shape
    size = two_c // 2
    pitch = two_c + 1
    step = pl.program_id(0)
    units = table_ref.shape[0] * table_ref.shape[1]
    span = sig * (two_c + 8)
    tables = table_ref.reshape(units, count * frames, 2 * LANES)
    for u in range(units):
        if first:
            fill_tables(tables, *makers, u)
        acc = None
        for n, part in enumerate(parts):
            term = jnp.dot(
                part[...].reshape(sig * two_c, frames),
                tables[u, n * frames : (n + 1) * frames],
                preferred_element_type=jnp.float32,
            )
            acc = term if acc is None else acc + term
        acc = acc.reshape(sig, 2, size, 2 * LANES)
        p, q = acc[..., :LANES], acc[..., LANES:]
        real, imag = p[:, 0] + q[:, 1], p[:, 1] - q[:, 0]
        for s in range(sig):
            zs[pl.ds(u * span + s * pitch, size), :] = real[s]
            zs[pl.ds(u * span + s * pitch + size, size), :] = imag[s]
    for n, out in enumerate(outs):

        @pl.when(step // steps == n)
        def _(out=out):
            for u in range(units):
                for c in range(size):
                    for part in range(2):
                        at = pl.ds(u * span + part * size + c, sig, stride=pitch)
                        out[u, c, part] = zs[at, :].astype(jnp.bfloat16)


def fine(parts, tables, turned, makers=None):
    sig, two_c, span = parts[0].shape
    frames = span * len(parts)
    first = makers is not None
    if first:
        dests = makers[2].shape[0]
        tables = jax.ShapeDtypeStruct((dests // 4, 4, frames, 2 * LANES), jnp.bfloat16)
    high, low = tables.shape[:2]
    unit = (two_c // 2, 2, sig, LANES)
    if turned:
        grid, units, count = low, high, 2
        spec = pl.BlockSpec((high, 1) + tables.shape[2:], lambda t: (0, t % 2 * 2 + t // 2, 0, 0))
    else:
        grid, units, count = high, low, high
        spec = pl.BlockSpec((1, low) + tables.shape[2:], lambda t: (t, 0, 0, 0))
    steps = grid // count

    def place(n):
        return lambda t: (jnp.clip(t - n * steps, 0, steps - 1), 0, 0, 0, 0)

    whole = [pl.BlockSpec(p.shape, lambda t: (0, 0, 0)) for p in parts]
    out_specs = [pl.BlockSpec((units,) + unit, place(n)) for n in range(count)]
    out_shape = [jax.ShapeDtypeStruct((steps * units,) + unit, jnp.bfloat16) for _ in range(count)]
    if first:
        kept = pl.BlockSpec(makers[0].shape, lambda t: (0, 0, 0))
        turn = pl.BlockSpec((low,) + makers[2].shape[1:], lambda t: (t, 0, 0))
        in_specs, operands = whole + [kept, kept, turn, turn], (*parts, *makers)
        out_specs, out_shape = out_specs + [spec], out_shape + [tables]
    else:
        in_specs, operands = whole + [spec], (*parts, tables)
    return pl.pallas_call(
        functools.partial(fine_kernel, steps, first, len(parts)),
        grid=(grid,),
        in_specs=in_specs,
        out_specs=out_specs,
        out_shape=out_shape,
        scratch_shapes=[pltpu.VMEM((units * sig * (two_c + 8), LANES), jnp.float32)],
        compiler_params=pltpu.CompilerParams(vmem_limit_bytes=VMEM),
        cost_estimate=pl.CostEstimate(
            flops=2 * sig * two_c * frames * high * low * 2 * LANES,
            bytes_accessed=3 * sig * two_c * frames + 4 * high * low * frames * LANES,
            transcendentals=0,
        ),
    )(*operands)


def pack_kernel(*refs):
    ins, out = refs[:-1], refs[-1]
    for n, ref in enumerate(ins):
        out[n] = ref[(0,) * (len(ref.shape) - 4)]


def pack(slots):
    size = slots[0][0].shape[-4]
    tail = slots[0][0].shape[-3:]
    half = size // 2
    return pl.pallas_call(
        pack_kernel,
        grid=(2,),
        in_specs=[
            pl.BlockSpec((1,) * len(at) + (half,) + tail, lambda c, at=at: at + (c, 0, 0, 0))
            for _, at in slots
        ],
        out_specs=pl.BlockSpec((len(slots), half) + tail, lambda c: (0, c, 0, 0, 0)),
        out_shape=jax.ShapeDtypeStruct((len(slots), size) + tail, jnp.bfloat16),
        compiler_params=pltpu.CompilerParams(vmem_limit_bytes=VMEM),
        cost_estimate=pl.CostEstimate(
            flops=0, bytes_accessed=4 * len(slots) * size * math.prod(tail), transcendentals=0
        ),
    )(*[array for array, _ in slots])


def correlate_kernel(sources, scale, per_q, me_ref, *refs):
    ins, out, xr, xi = refs[: len(sources)], refs[-3], refs[-2], refs[-1]
    me = me_ref[0]
    for ref, units in zip(ins, sources):
        for at, rel in units:
            row = pl.ds(pl.multiple_of((me ^ rel) * ROWS, ROWS), ROWS)
            for c in range(out.shape[0]):
                xr[c, row, :] = ref[at + (c, 0)]
                xi[c, row, :] = ref[at + (c, 1)]
    lane = lax.broadcasted_iota(jnp.int32, (1, LANES), 1)
    zero = jnp.zeros((), jnp.bfloat16)
    picks = [lane // per_q == q for q in range(LANES // per_q)]
    dims = (((1,), (1,)), ((), ()))

    def body(c, _):
        re, im = xr[c], xi[c]
        for part in range(2):
            right = jnp.concatenate([-im, re] if part else [re, im], axis=1)
            for q, pick in enumerate(picks):
                left = jnp.concatenate([jnp.where(pick, re, zero), jnp.where(pick, im, zero)], axis=1)
                vis = lax.dot_general(left, right, dims, preferred_element_type=jnp.float32)
                out[c, q, part] = (vis * scale).astype(jnp.bfloat16)
        return 0

    lax.fori_loop(0, out.shape[0], body, 0)


def correlate_chunk(me, arrays, leads, sources, whole, offset, shape, per_q, scale):
    size = arrays[0].shape[-4]
    signals = shape[-1]
    specs = [pl.BlockSpec(memory_space=pltpu.SMEM)]
    for a, lead in zip(arrays, leads):
        specs.append(
            pl.BlockSpec(
                tuple(lead) + (GROUP,) + a.shape[-3:],
                lambda c, n=len(lead): (0,) * n + (c, 0, 0, 0),
            )
        )
    operands = [me] + list(arrays)
    alias = {}
    if whole is not None:
        alias = {len(operands): 0}
        specs.append(pl.BlockSpec(memory_space=pl.ANY))
        operands.append(whole)
    return pl.pallas_call(
        functools.partial(correlate_kernel, sources, scale, per_q),
        grid=(size // GROUP,),
        in_specs=specs,
        out_specs=pl.BlockSpec((GROUP,) + shape[1:], lambda c: (c + offset // GROUP, 0, 0, 0, 0)),
        out_shape=jax.ShapeDtypeStruct(shape, jnp.bfloat16),
        scratch_shapes=[pltpu.VMEM((GROUP, signals, LANES), jnp.bfloat16)] * 2,
        input_output_aliases=alias,
        compiler_params=pltpu.CompilerParams(vmem_limit_bytes=VMEM),
        cost_estimate=pl.CostEstimate(
            flops=size * 8 * signals * signals * 4 * LANES,
            bytes_accessed=size * 2 * math.prod(shape[1:]),
            transcendentals=0,
        ),
    )(*operands)


def chunk_sizes(channels):
    eighth = channels // 8
    return [eighth, 2 * eighth, 2 * eighth, 2 * eighth, eighth]


DIRECT = 3


def per_device(samples, coarse_taps, fine_taps):
    sig, samp = samples.shape
    taps_n, frame_len = coarse_taps.shape
    ftaps_n, fine_len = fine_taps.shape
    dests = lax.axis_size("sta")
    me = lax.axis_index("sta")
    win = lax.axis_index("win")
    frames = samp // frame_len
    fine_local = frames // fine_len
    total = fine_local * 2
    per_dest = fine_len // dests
    channels = KEEP // 2
    chunks = chunk_sizes(channels)
    low = 4
    high = dests // low

    dft = coarse_rows(frame_len, channels, chunks)
    side = win[None].astype(jnp.int32)
    blocks = frames // BLOCK
    half = blocks // 2
    later = coarse(side, samples, (), coarse_taps, dft, chunks, half, blocks - half)
    hist = from_behind(samples[:, samp - (taps_n - 1) * frame_len :], "win", 1)
    early = coarse(side, samples, (hist,), coarse_taps, dft, chunks, 0, half)
    count = len(chunks)
    own = [(early[k], later[k]) for k in range(count)]
    away = [(early[count + k], later[count + k]) for k in range(count)]

    lane = jnp.arange(LANES, dtype=jnp.int32)
    frame_of = lane % total
    weights = fine_taps.astype(jnp.float32)

    def taps_table(side):
        block = side * fine_local + jnp.arange(fine_local, dtype=jnp.int32)
        late = frame_of[None, :] - block[:, None]
        table = jnp.zeros((fine_local, fine_len, LANES), jnp.float32)
        for m in range(ftaps_n):
            table = table + jnp.where((late == m)[:, None, :], weights[m][None, :, None], 0.0)
        return table

    fine_of = (me ^ jnp.arange(dests, dtype=jnp.int32))[:, None] * per_dest + (lane // total)[None, :]
    turns = fine_of[:, None, :] * jnp.arange(fine_len, dtype=jnp.int32)[None, :, None]
    angles = (turns % fine_len).astype(jnp.float32) * (2.0 * math.pi / fine_len)
    makers = (taps_table(win), taps_table(1 - win), jnp.cos(angles), jnp.sin(angles))

    shape = (channels, per_dest, 2, sig * dests, sig * dests)
    highs = range(high)
    oths = [[swap(part, "win", 1) for part in away[k]] for k in range(count)]

    pieces = []
    for k in range(len(chunks)):
        if k == 0:
            *sent, tables = fine((*own[k], *oths[k]), None, False, makers)
        else:
            sent = fine((*own[k], *oths[k]), tables, k >= DIRECT)
        if k < DIRECT:
            held = [sent[0]] + [swap(sent[n], "sta", low * n) for n in highs if n]
            block = pack([(h, (2 + c,)) for c in range(2) for h in held])
            over = swap(block, "sta", 2)
            block = pack([(h, (1,)) for h in held] + [(over, (high + n,)) for n in highs])
            last = swap(block, "sta", 1)
            arrays = held + [over, last]
            leads = [(1,)] * high + [(high,), (2 * high,)]
            sources = [[((0,), low * n)] for n in highs]
            sources.append([((n,), low * n + 2) for n in highs])
            sources.append([((y * high + n,), low * n + 2 * y + 1) for y in range(2) for n in highs])
        else:
            near, pair = sent[0], swap(sent[1], "sta", 1)
            block = pack([(a, (high + n,)) for n in highs for a in (near, pair)])
            over = swap(block, "sta", 2)
            arrays, leads = [near, pair, over], [(1,), (1,), (2,)]
            sources = [[((0,), 0)], [((0,), 1)], [((c,), 2 + c) for c in range(2)]]
            for n in highs:
                if n:
                    slots = [(near, (n,)), (pair, (n,)), (over, (2 * n,)), (over, (2 * n + 1,))]
                    block = pack(slots)
                    arrays.append(swap(block, "sta", low * n))
                    leads.append((low,))
                    sources.append([((b,), low * n + b) for b in range(low)])
        pieces.append((arrays, leads, sources))
    result = None
    who = me[None].astype(jnp.int32)
    for k in range(len(chunks)):
        result = correlate_chunk(
            who, *pieces[k], result, sum(chunks[:k]), shape, total, 1.0 / total
        )
    return result


def serves(mesh, samples, coarse_taps, fine_taps):
    wins, stas = mesh.shape["win"], mesh.shape["sta"]
    sig, samp = samples.shape[0] // stas, samples.shape[1] // wins
    taps_n, frame_len = coarse_taps.shape
    fine_len = fine_taps.shape[1]
    frames = samp // frame_len
    return (
        wins == 2
        and stas % 4 == 0
        and stas & (stas - 1) == 0
        and sig == ROWS
        and taps_n == ROWS
        and frame_len % WIDE == 0
        and frames % (2 * BLOCK) == 0
        and frames % fine_len == 0
        and fine_len % stas == 0
        and fine_len // stas * (2 * frames // fine_len) == LANES
    )


def solution(mesh):
    placed = (P("sta", "win"), P(), P())

    def step(samples, coarse_taps, fine_taps):
        own_path = serves(mesh, samples, coarse_taps, fine_taps)

        def body(*args):
            if not own_path:
                return per_device_general(*args)
            return per_device(*args)

        f = jax.shard_map(
            body,
            mesh=mesh,
            in_specs=placed,
            out_specs=P("win", "sta", None, None, None),
            check_vma=False,
        )
        return f(samples, coarse_taps, fine_taps)

    return step
```

```python
import functools
import math

import jax
import jax.numpy as jnp
import numpy as np
from jax import lax
from jax.experimental import pallas as pl
from jax.experimental.pallas import tpu as pltpu
from jax.sharding import PartitionSpec as P

KEEP = 128
LANES = 128
WIDE = 256
PITCH = 17
GROUP = 4
VMEM = 63 << 20
ROWS = 16
BLOCK = 128


def from_behind(x, axis, by):
    size = lax.axis_size(axis)
    pairs = [(i, i + by) for i in range(size) if 0 <= i + by < size]
    return lax.ppermute(x, axis, pairs)


def coarse_matrix(frame_len, band_count):
    channels = frame_len // 8 + jnp.arange(band_count, dtype=jnp.int32)
    products = jnp.arange(frame_len, dtype=jnp.int32)[:, None] * channels[None, :]
    angles = (products % frame_len).astype(jnp.float32) * (2.0 * math.pi / frame_len)
    return jnp.concatenate([jnp.cos(angles), -jnp.sin(angles)], axis=1).astype(jnp.bfloat16)


def fine_tables(fine_len):
    products = (
        jnp.arange(fine_len, dtype=jnp.int32)[:, None]
        * jnp.arange(fine_len, dtype=jnp.int32)[None, :]
    )
    angles = (products % fine_len).astype(jnp.float32) * (2.0 * math.pi / fine_len)
    return (jnp.cos(angles), jnp.sin(angles))


def correlate(spectra_in, pieces):
    band_local, fine_local, sig_count, columns = spectra_in.shape
    split_view = spectra_in.reshape(
        band_local, fine_local, sig_count, pieces, 2, columns // (2 * pieces)
    )
    turned = jnp.stack([split_view[:, :, :, :, 1], -split_view[:, :, :, :, 0]], axis=4).reshape(
        band_local, fine_local, sig_count, columns
    )
    real_vis = jnp.einsum(
        "kqsc,kqtc->kqst", spectra_in, spectra_in, preferred_element_type=jnp.float32
    )
    imag_vis = jnp.einsum("kqsc,kqtc->kqst", turned, spectra_in, preferred_element_type=jnp.float32)
    return jnp.stack([real_vis, imag_vis], axis=2)


def per_device_general(samples, coarse_taps, fine_taps):
    sig_local, samp_local = samples.shape
    tap_count, frame_len = coarse_taps.shape
    fine_tap_count, fine_len = fine_taps.shape
    band_count = KEEP
    frame_count = samp_local // frame_len
    frames_local = samples.reshape(sig_local, frame_count, frame_len)
    earlier = from_behind(frames_local[:, frame_count - (tap_count - 1) :], "win", 1)
    padded = jnp.concatenate([earlier, frames_local], axis=1)
    windowed = jnp.zeros((sig_local, frame_count, frame_len), jnp.float32)
    for tap_index in range(tap_count):
        start = tap_count - 1 - tap_index
        windowed = windowed + coarse_taps[tap_index].astype(jnp.float32)[None, None, :] * padded[
            :, start : start + frame_count
        ].astype(jnp.float32)
    spectra = jnp.dot(
        windowed.astype(jnp.bfloat16).reshape(sig_local * frame_count, frame_len),
        coarse_matrix(frame_len, band_count),
        preferred_element_type=jnp.float32,
    )
    spectra = spectra.astype(jnp.bfloat16).reshape(sig_local, frame_count, 2 * band_count)
    history = (fine_tap_count - 1) * fine_len
    carried = from_behind(spectra[:, frame_count - history :], "win", 1)
    extended = jnp.concatenate([carried, spectra], axis=1)
    fine_count = frame_count // fine_len
    groups = extended.reshape(sig_local, fine_count + fine_tap_count - 1, fine_len, 2, band_count)
    filtered = jnp.zeros((sig_local, fine_count, fine_len, 2, band_count), jnp.float32)
    for tap_index in range(fine_tap_count):
        start = fine_tap_count - 1 - tap_index
        filtered = filtered + fine_taps[tap_index].astype(jnp.float32)[
            None, None, :, None, None
        ] * groups[:, start : start + fine_count].astype(jnp.float32)
    cosines, sines = fine_tables(fine_len)
    real_part = filtered[:, :, :, 0]
    imag_part = filtered[:, :, :, 1]
    highest = lax.Precision.HIGHEST
    out_real = jnp.einsum("qj,sgjk->kqsg", cosines, real_part, precision=highest) + jnp.einsum(
        "qj,sgjk->kqsg", sines, imag_part, precision=highest
    )
    out_imag = jnp.einsum("qj,sgjk->kqsg", cosines, imag_part, precision=highest) - jnp.einsum(
        "qj,sgjk->kqsg", sines, real_part, precision=highest
    )
    local_spectra = (
        jnp.stack([out_real, out_imag], axis=3)
        .astype(jnp.bfloat16)
        .reshape(band_count, fine_len, sig_local, 2 * fine_count)
    )
    frame_total = fine_count * lax.axis_size("win")
    moved = lax.all_to_all(local_spectra, "sta", split_axis=1, concat_axis=2, tiled=True)
    moved = lax.all_to_all(moved, "win", split_axis=0, concat_axis=3, tiled=True)
    vis_local = correlate(moved, lax.axis_size("win"))
    return (vis_local / frame_total).astype(jnp.bfloat16)


def swap(x, axis, by):
    return lax.ppermute(x, axis, [(i, i ^ by) for i in range(lax.axis_size(axis))])


def coarse_rows(frame_len, band_half, chunks):
    rows = []
    for h in range(2):
        base = frame_len // 8 + h * band_half
        for size in chunks:
            channel = np.arange(base, base + size, dtype=np.int32)
            products = channel[:, None] * np.arange(frame_len, dtype=np.int32)[None, :]
            angles = (products % frame_len).astype(np.float32) * np.float32(2.0 * math.pi / frame_len)
            rows += [np.cos(angles), -np.sin(angles)]
            base += size
    return np.concatenate(rows).reshape(2, 2 * band_half, frame_len).astype(jnp.bfloat16)


def coarse_kernel(chunks, taps_n, win_ref, x_ref, before_ref, taps_ref, dft_ref, *refs):
    opening = len(refs) > 3 + 2 * len(chunks)
    hist_ref, refs = (refs[0], refs[1:]) if opening else (None, refs)
    outs, (xs, even, odd) = refs[:-3], refs[-3:]
    step, last = pl.program_id(0), pl.num_programs(0) - 1
    keep = taps_n - 1
    pieces = xs.shape[1]
    skip = before_ref.shape[1] // (pieces * WIDE) - keep
    group = 8

    def load():
        def put(ref, gap):
            for f in range(keep):
                for j in range(pieces):
                    at = ((f + gap) * pieces + j) * WIDE
                    xs[f, j] = ref[:, at : at + WIDE]

        if opening:
            pl.when(step == 0)(lambda: put(hist_ref, 0))
            pl.when(step > 0)(lambda: put(before_ref, skip))
        else:
            put(before_ref, skip)

        def move(f, _):
            for j in range(pieces):
                at = pl.multiple_of((f * pieces + j) * WIDE, WIDE)
                xs[keep + f, j] = x_ref[:, pl.ds(at, WIDE)]
            return 0

        lax.fori_loop(0, BLOCK, move, 0, unroll=8)

    def fir(wd, first, j):
        taps = [taps_ref[j, m] for m in range(taps_n)]
        xv = [xs[first + t, j] for t in range(group + keep)]
        for g in range(group):
            terms = [taps[m] * xv[g + keep - m] for m in range(taps_n)]
            for _ in range(2):
                terms = [a + b for a, b in zip(terms[::2], terms[1::2])]
            wide = [t.astype(jnp.float32) for t in terms]
            while len(wide) > 1:
                wide = [a + b for a, b in zip(wide[::2], wide[1::2])]
            rows = pl.ds((first + g) * PITCH, ROWS)
            for n in range(WIDE // LANES):
                wd[j * (WIDE // LANES) + n, rows, :] = wide[0][:, n * LANES : (n + 1) * LANES]

    def project(wd, p):
        rows = []
        for t in range(2):
            parts = [wd[j, pl.ds(2 * p + t, BLOCK, stride=PITCH), :] for j in range(wd.shape[0])]
            rows.append(jnp.concatenate(parts, axis=1).astype(jnp.bfloat16))
        both = jnp.concatenate(rows, axis=0)
        mine = win_ref[0]
        matrix = jnp.concatenate([dft_ref[mine], dft_ref[1 - mine]], axis=0)
        res = lax.dot_general(
            matrix, both, (((1,), (1,)), ((), ())), preferred_element_type=jnp.float32
        ).astype(jnp.bfloat16)
        for t in range(2):
            base = 0
            for n, out in enumerate(outs):
                size = 2 * chunks[n % len(chunks)]
                out[2 * p + t] = res[base : base + size, t * BLOCK : (t + 1) * BLOCK]
                base += size

    pairs = ROWS // 2
    share = BLOCK // pairs // group

    def run(fill, drain):
        def body(p, _):
            if drain is not None:
                project(drain, p)
            if fill is not None:
                for n in range(share):
                    for j in range(pieces):
                        fir(fill, (p * share + n) * group, j)
            return 0

        if fill is not None:
            load()
        lax.fori_loop(0, pairs, body, 0)

    @pl.when(step == 0)
    def _():
        run(even, None)

    @pl.when((step > 0) & (step < last) & (step % 2 == 1))
    def _():
        run(odd, even)

    @pl.when((step > 0) & (step < last) & (step % 2 == 0))
    def _():
        run(even, odd)

    @pl.when((step == last) & (step % 2 == 1))
    def _():
        run(None, even)

    @pl.when((step == last) & (step % 2 == 0))
    def _():
        run(None, odd)


def coarse(win, samples, hist, coarse_taps, dft, chunks, start, blocks):
    sig, _ = samples.shape
    taps_n, frame_len = coarse_taps.shape
    pieces = frame_len // WIDE
    frames = blocks * BLOCK
    before = taps_n
    taps = jnp.broadcast_to(
        coarse_taps.reshape(taps_n, pieces, WIDE).transpose(1, 0, 2)[:, :, None],
        (pieces, taps_n, ROWS, WIDE),
    )
    ratio = BLOCK // before
    shapes = [jax.ShapeDtypeStruct((sig, 2 * c, frames), jnp.bfloat16) for c in chunks * 2]

    def at(i):
        return start + jnp.minimum(i, blocks - 1)

    return pl.pallas_call(
        functools.partial(coarse_kernel, chunks, taps_n),
        grid=(blocks + 1,),
        in_specs=[
            pl.BlockSpec(memory_space=pltpu.SMEM),
            pl.BlockSpec((sig, BLOCK * frame_len), lambda i: (0, at(i))),
            pl.BlockSpec((sig, before * frame_len), lambda i: (0, jnp.maximum(at(i) * ratio - 1, 0))),
            pl.BlockSpec(taps.shape, lambda i: (0, 0, 0, 0)),
            pl.BlockSpec(dft.shape, lambda i: (0, 0, 0)),
        ]
        + [pl.BlockSpec(h.shape, lambda i: (0, 0)) for h in hist],
        out_specs=[
            pl.BlockSpec((sig, 2 * c, BLOCK), lambda i: (0, 0, jnp.maximum(i - 1, 0)))
            for c in chunks * 2
        ],
        out_shape=shapes,
        scratch_shapes=[pltpu.VMEM((BLOCK + taps_n - 1, pieces, sig, WIDE), jnp.bfloat16)]
        + [pltpu.VMEM((frame_len // LANES, BLOCK * PITCH, LANES), jnp.float32)] * 2,
        compiler_params=pltpu.CompilerParams(vmem_limit_bytes=VMEM),
        cost_estimate=pl.CostEstimate(
            flops=2 * sig * frames * frame_len * (dft.shape[0] * dft.shape[1] + 128 * taps_n),
            bytes_accessed=4 * sig * frames * frame_len,
            transcendentals=0,
        ),
    )(win, samples, samples, taps, dft, *hist)


def fill_tables(tables, town_ref, toth_ref, cos_ref, sin_ref, u, dest):
    fine_local, fine_len, _ = town_ref.shape
    frames = fine_local * fine_len
    for side, t_ref in enumerate((town_ref, toth_ref)):
        for part, turn in enumerate((cos_ref[dest], sin_ref[dest])):
            rows = (t_ref[...] * turn).astype(jnp.bfloat16).reshape(frames, LANES)
            tables[u, side * frames : (side + 1) * frames, part * LANES : (part + 1) * LANES] = rows


def fine_kernel(steps, first, count, *refs):
    parts, refs = refs[:count], refs[count:]
    if first:
        me, makers, outs, table_ref, zs = refs[0][0], refs[1:5], refs[5:-2], refs[-2], refs[-1]
    else:
        table_ref, outs, zs = refs[0], refs[1:-1], refs[-1]
    sig, two_c, _ = parts[0].shape
    spans = [part.shape[2] for part in parts]
    frames = sum(spans)
    size = two_c // 2
    pitch = two_c + 1
    step = pl.program_id(0)
    units = table_ref.shape[0] * table_ref.shape[1]
    span = sig * (two_c + 8)
    tables = table_ref.reshape(units, frames, 2 * LANES)
    for u in range(units):
        if first:
            fill_tables(tables, *makers, u, me ^ (step * units + u))
        acc = None
        for n, part in enumerate(parts):
            term = jnp.dot(
                part[...].reshape(sig * two_c, spans[n]),
                tables[u, sum(spans[:n]) : sum(spans[: n + 1])],
                preferred_element_type=jnp.float32,
            )
            acc = term if acc is None else acc + term
        acc = acc.reshape(sig, 2, size, 2 * LANES)
        p, q = acc[..., :LANES], acc[..., LANES:]
        real, imag = p[:, 0] + q[:, 1], p[:, 1] - q[:, 0]
        for s in range(sig):
            zs[pl.ds(u * span + s * pitch, size), :] = real[s]
            zs[pl.ds(u * span + s * pitch + size, size), :] = imag[s]
    for n, out in enumerate(outs):

        @pl.when(step // steps == n)
        def _(out=out):
            for u in range(units):
                for c in range(size):
                    for part in range(2):
                        at = pl.ds(u * span + part * size + c, sig, stride=pitch)
                        out[u, c, part] = zs[at, :].astype(jnp.bfloat16)


def fine(parts, tables, turned, makers=None):
    sig, two_c, _ = parts[0].shape
    frames = sum(p.shape[2] for p in parts)
    first = makers is not None
    if first:
        dests = makers[3].shape[0]
        tables = jax.ShapeDtypeStruct((dests // 4, 4, frames, 2 * LANES), jnp.bfloat16)
    high, low = tables.shape[:2]
    unit = (two_c // 2, 2, sig, LANES)
    if turned:
        grid, units, count = low, high, 2
        spec = pl.BlockSpec((high, 1) + tables.shape[2:], lambda t: (0, t % 2 * 2 + t // 2, 0, 0))
    else:
        grid, units, count = high, low, high
        spec = pl.BlockSpec((1, low) + tables.shape[2:], lambda t: (t, 0, 0, 0))
    steps = grid // count

    def place(n):
        return lambda t: (jnp.clip(t - n * steps, 0, steps - 1), 0, 0, 0, 0)

    whole = [pl.BlockSpec(p.shape, lambda t: (0, 0, 0)) for p in parts]
    out_specs = [pl.BlockSpec((units,) + unit, place(n)) for n in range(count)]
    out_shape = [jax.ShapeDtypeStruct((steps * units,) + unit, jnp.bfloat16) for _ in range(count)]
    if first:
        kept = [pl.BlockSpec(m.shape, lambda t: (0, 0, 0)) for m in makers[1:]]
        in_specs = whole + [pl.BlockSpec(memory_space=pltpu.SMEM)] + kept
        operands = (*parts, *makers)
        out_specs, out_shape = out_specs + [spec], out_shape + [tables]
    else:
        in_specs, operands = whole + [spec], (*parts, tables)
    return pl.pallas_call(
        functools.partial(fine_kernel, steps, first, len(parts)),
        grid=(grid,),
        in_specs=in_specs,
        out_specs=out_specs,
        out_shape=out_shape,
        scratch_shapes=[pltpu.VMEM((units * sig * (two_c + 8), LANES), jnp.float32)],
        compiler_params=pltpu.CompilerParams(vmem_limit_bytes=VMEM),
        cost_estimate=pl.CostEstimate(
            flops=2 * sig * two_c * frames * high * low * 2 * LANES,
            bytes_accessed=3 * sig * two_c * frames + 4 * high * low * frames * LANES,
            transcendentals=0,
        ),
    )(*operands)


def pack_kernel(*refs):
    ins, out = refs[:-1], refs[-1]
    for n, ref in enumerate(ins):
        out[n] = ref[(0,) * (len(ref.shape) - 4)]


def pack(slots):
    size = slots[0][0].shape[-4]
    tail = slots[0][0].shape[-3:]
    half = size // 2
    return pl.pallas_call(
        pack_kernel,
        grid=(2,),
        in_specs=[
            pl.BlockSpec((1,) * len(at) + (half,) + tail, lambda c, at=at: at + (c, 0, 0, 0))
            for _, at in slots
        ],
        out_specs=pl.BlockSpec((len(slots), half) + tail, lambda c: (0, c, 0, 0, 0)),
        out_shape=jax.ShapeDtypeStruct((len(slots), size) + tail, jnp.bfloat16),
        compiler_params=pltpu.CompilerParams(vmem_limit_bytes=VMEM),
        cost_estimate=pl.CostEstimate(
            flops=0, bytes_accessed=4 * len(slots) * size * math.prod(tail), transcendentals=0
        ),
    )(*[array for array, _ in slots])


def correlate_kernel(sources, scale, per_q, me_ref, *refs):
    ins, out, xr, xi = refs[: len(sources)], refs[-3], refs[-2], refs[-1]
    me = me_ref[0]
    for ref, units in zip(ins, sources):
        for at, rel in units:
            row = pl.ds(pl.multiple_of((me ^ rel) * ROWS, ROWS), ROWS)
            for c in range(out.shape[0]):
                xr[c, row, :] = ref[at + (c, 0)]
                xi[c, row, :] = ref[at + (c, 1)]
    lane = lax.broadcasted_iota(jnp.int32, (1, LANES), 1)
    zero = jnp.zeros((), jnp.bfloat16)
    picks = [lane // per_q == q for q in range(LANES // per_q)]
    dims = (((1,), (1,)), ((), ()))

    def body(c, _):
        re, im = xr[c], xi[c]
        for part in range(2):
            right = jnp.concatenate([-im, re] if part else [re, im], axis=1)
            for q, pick in enumerate(picks):
                left = jnp.concatenate([jnp.where(pick, re, zero), jnp.where(pick, im, zero)], axis=1)
                vis = lax.dot_general(left, right, dims, preferred_element_type=jnp.float32)
                out[c, q, part] = (vis * scale).astype(jnp.bfloat16)
        return 0

    lax.fori_loop(0, out.shape[0], body, 0)


def correlate_chunk(me, arrays, leads, sources, whole, offset, shape, per_q, scale):
    size = arrays[0].shape[-4]
    signals = shape[-1]
    specs = [pl.BlockSpec(memory_space=pltpu.SMEM)]
    for a, lead in zip(arrays, leads):
        specs.append(
            pl.BlockSpec(
                tuple(lead) + (GROUP,) + a.shape[-3:],
                lambda c, n=len(lead): (0,) * n + (c, 0, 0, 0),
            )
        )
    operands = [me] + list(arrays)
    alias = {}
    if whole is not None:
        alias = {len(operands): 0}
        specs.append(pl.BlockSpec(memory_space=pl.ANY))
        operands.append(whole)
    return pl.pallas_call(
        functools.partial(correlate_kernel, sources, scale, per_q),
        grid=(size // GROUP,),
        in_specs=specs,
        out_specs=pl.BlockSpec((GROUP,) + shape[1:], lambda c: (c + offset // GROUP, 0, 0, 0, 0)),
        out_shape=jax.ShapeDtypeStruct(shape, jnp.bfloat16),
        scratch_shapes=[pltpu.VMEM((GROUP, signals, LANES), jnp.bfloat16)] * 2,
        input_output_aliases=alias,
        compiler_params=pltpu.CompilerParams(vmem_limit_bytes=VMEM),
        cost_estimate=pl.CostEstimate(
            flops=size * 8 * signals * signals * 4 * LANES,
            bytes_accessed=size * 2 * math.prod(shape[1:]),
            transcendentals=0,
        ),
    )(*operands)


def chunk_sizes(channels):
    eighth = channels // 8
    return [eighth, 2 * eighth, 2 * eighth, 2 * eighth, eighth]


DIRECT = 3


def per_device(samples, coarse_taps, fine_taps):
    sig, samp = samples.shape
    taps_n, frame_len = coarse_taps.shape
    ftaps_n, fine_len = fine_taps.shape
    dests = lax.axis_size("sta")
    me = lax.axis_index("sta")
    win = lax.axis_index("win")
    frames = samp // frame_len
    fine_local = frames // fine_len
    total = fine_local * 2
    per_dest = fine_len // dests
    channels = KEEP // 2
    chunks = chunk_sizes(channels)
    low = 4
    high = dests // low

    dft = coarse_rows(frame_len, channels, chunks)
    side = win[None].astype(jnp.int32)
    blocks = frames // BLOCK
    opening = blocks // 2
    later = coarse(side, samples, (), coarse_taps, dft, chunks, opening, blocks - opening)
    hist = from_behind(samples[:, samp - (taps_n - 1) * frame_len :], "win", 1)
    early = coarse(side, samples, (hist,), coarse_taps, dft, chunks, 0, opening)
    count = len(chunks)
    own = [(early[k], later[k]) for k in range(count)]
    away = [(early[count + k], later[count + k]) for k in range(count)]

    lane = jnp.arange(LANES, dtype=jnp.int32)
    frame_of = lane % total
    weights = fine_taps.astype(jnp.float32)

    def taps_table(side):
        block = side * fine_local + jnp.arange(fine_local, dtype=jnp.int32)
        late = frame_of[None, :] - block[:, None]
        table = jnp.zeros((fine_local, fine_len, LANES), jnp.float32)
        for m in range(ftaps_n):
            table = table + jnp.where((late == m)[:, None, :], weights[m][None, :, None], 0.0)
        return table

    spot = np.arange(LANES, dtype=np.int32)
    fine_of = np.arange(dests, dtype=np.int32)[:, None] * per_dest + (spot // total)[None, :]
    turns = fine_of[:, None, :] * np.arange(fine_len, dtype=np.int32)[None, :, None]
    angles = (turns % fine_len).astype(np.float32) * np.float32(2.0 * math.pi / fine_len)
    who = me[None].astype(jnp.int32)
    makers = (who, taps_table(win), taps_table(1 - win), np.cos(angles), np.sin(angles))

    shape = (channels, per_dest, 2, sig * dests, sig * dests)
    highs = range(high)
    oths = [[swap(part, "win", 1) for part in away[k]] for k in range(count)]

    pieces = []
    for k in range(len(chunks)):
        if k == 0:
            *sent, tables = fine((*own[k], *oths[k]), None, False, makers)
        else:
            sent = fine((*own[k], *oths[k]), tables, k >= DIRECT)
        if k < DIRECT:
            held = [sent[0]] + [swap(sent[n], "sta", low * n) for n in highs if n]
            block = pack([(h, (2 + c,)) for c in range(2) for h in held])
            over = swap(block, "sta", 2)
            block = pack([(h, (1,)) for h in held] + [(over, (high + n,)) for n in highs])
            last = swap(block, "sta", 1)
            arrays = held + [over, last]
            leads = [(1,)] * high + [(high,), (2 * high,)]
            sources = [[((0,), low * n)] for n in highs]
            sources.append([((n,), low * n + 2) for n in highs])
            sources.append([((y * high + n,), low * n + 2 * y + 1) for y in range(2) for n in highs])
        else:
            near, pair = sent[0], swap(sent[1], "sta", 1)
            block = pack([(a, (high + n,)) for n in highs for a in (near, pair)])
            over = swap(block, "sta", 2)
            arrays, leads = [near, pair, over], [(1,), (1,), (2,)]
            sources = [[((0,), 0)], [((0,), 1)], [((c,), 2 + c) for c in range(2)]]
            for n in highs:
                if n:
                    slots = [(near, (n,)), (pair, (n,)), (over, (2 * n,)), (over, (2 * n + 1,))]
                    block = pack(slots)
                    arrays.append(swap(block, "sta", low * n))
                    leads.append((low,))
                    sources.append([((b,), low * n + b) for b in range(low)])
        pieces.append((arrays, leads, sources))
    result = None
    for k in range(len(chunks)):
        result = correlate_chunk(
            who, *pieces[k], result, sum(chunks[:k]), shape, total, 1.0 / total
        )
    return result


def serves(mesh, samples, coarse_taps, fine_taps):
    wins, stas = mesh.shape["win"], mesh.shape["sta"]
    sig, samp = samples.shape[0] // stas, samples.shape[1] // wins
    taps_n, frame_len = coarse_taps.shape
    fine_len = fine_taps.shape[1]
    frames = samp // frame_len
    return (
        wins == 2
        and stas % 4 == 0
        and stas & (stas - 1) == 0
        and sig == ROWS
        and taps_n == ROWS
        and frame_len % WIDE == 0
        and frames % (4 * BLOCK) == 0
        and frames % fine_len == 0
        and fine_len % stas == 0
        and fine_len // stas * (2 * frames // fine_len) == LANES
    )


def solution(mesh):
    placed = (P("sta", "win"), P(), P())

    def step(samples, coarse_taps, fine_taps):
        own_path = serves(mesh, samples, coarse_taps, fine_taps)

        def body(*args):
            if not own_path:
                return per_device_general(*args)
            return per_device(*args)

        f = jax.shard_map(
            body,
            mesh=mesh,
            in_specs=placed,
            out_specs=P("win", "sta", None, None, None),
            check_vma=False,
        )
        return f(samples, coarse_taps, fine_taps)

    return step
```
